32 devices in a mesh: groups: 2 (over y), patch: 8 (over z, x), req: 2 (over core).
Axes of the slice: x: 2, y: 2, z: 4, core: 2. Of those that a mesh axis runs over, the one named last changes fastest.
Arguments:
- hidden: float32 [16, 8, 64, 1280], P(('groups', 'req'), 'patch'), parts along dimension 0
- skip: float32 [16, 8, 64, 1280], P(('groups', 'req'), 'patch'), parts along dimension 0, may hold values from -6 to 6
- timestep_embedding_table: float32 [50, 1280], replicated, may hold values from -5 to 5
- timesteps: int32 [16], P(('groups', 'req')), parts along dimension 0, may hold values from 0 to 49, as said below
- group_norm_gain: float32 [1280], replicated, may hold values from 0.1 to 1.9
- group_norm_bias: float32 [1280], replicated, may hold values from -3 to 3
- kernel_weight: bfloat16 [9, 1280, 1280], P(None, 'patch', 'req'), may hold values from -0.0546875 to 0.0546875
- adapter_down_weight: bfloat16 [32, 64, 11520], P(('groups', 'patch')), parts along dimension 0, may hold values from -0.0546875 to 0.0546875
- adapter_up_weight: bfloat16 [32, 64, 1280], P(('groups', 'patch')), parts along dimension 0, may hold values from -0.75 to 0.75
- request_adapter: int32 [16], P(('groups', 'req')), parts along dimension 0, may hold values from 0 to 15
- adapter_row_table: int32 [32], P('groups'), parts along dimension 0, may hold values from 0 to 15, each once
Outputs:
- block_out: float32 [16, 8, 64, 1280], P(('groups', 'req'), 'patch'), parts along dimension 0
The draws below stay inside these ranges and needn't reach their ends.
There are 2 independent parts, one for each index of `groups`. The reference program is written for one: setup_inputs(seed, part) draws one part's arguments, and reference() takes and returns one part's arrays. A program takes and returns all parts, laid end to end along the dimension named above; an argument that names none is the same for every part. Nothing has to cross between parts.
Inputs may be any that keep to these rules, and one draw needn't show every extreme that they name: adapter_row_table[a] is the store row of adapter a; every row is used once. Requests 0 and 1 have different timesteps.
All inputs are finite; a program needn't handle non-finite values.
Results may differ from the reference program's by a relative error of at most 0.0026.
Values may be sent and summed in bfloat16 or wider, within the bound.
A program may use at most 128 MiB of HBM per device.

```python
import math
import jax
import jax.numpy as jnp
import numpy as np
from jax import lax

CHANNEL_COUNT = 1280
GROUPS = 32
ADAPTER_RANK = 64
W = 64
STEPS = 50
H = 8
REQUESTS = 8
ADAPTER_COUNT = 16


def draw_hidden(key, part):
    key_base = jax.random.fold_in(key, 11)
    key_chan = jax.random.fold_in(key, 12)
    base = jax.random.normal(key_base, (REQUESTS, H, W, CHANNEL_COUNT), jnp.float32)
    row_scale = 3.0 ** (jnp.arange(H, dtype=jnp.float32) / max(H - 1, 1))
    chan_scale = jnp.exp(jax.random.uniform(key_chan, (CHANNEL_COUNT,), jnp.float32, -0.7, 0.7))
    return base * row_scale[None, :, None, None] * chan_scale[None, None, None, :]


def draw_timesteps(key, part):
    key_all = jax.random.fold_in(key, 21)
    key_off = jax.random.fold_in(key, 22)
    values = jax.random.randint(key_all, (REQUESTS,), 0, STEPS, dtype=jnp.int32)
    offset = jax.random.randint(key_off, (), 0, STEPS - 1, dtype=jnp.int32)
    second = (values[0] + 1 + offset) % STEPS
    return values.at[1].set(second.astype(jnp.int32))


def plant(entries, rng, low, top_value):
    longest = entries.shape.index(max(entries.shape))
    spots = []
    for shift in (0, 1):
        where = [jax.random.randint(jax.random.fold_in(rng, axis), (), 0, length) for axis, length in enumerate(entries.shape)]
        where[longest] = (where[longest] + shift) % entries.shape[longest]
        spots.append(tuple(where))
    return entries.at[spots[0]].set(low).at[spots[1]].set(top_value)


def shard_levels(rng, dims, shards, least, top_value):
    factor_of, own = 1.0, jax.random.fold_in(rng, 6)
    for axis_at, shards_of in shards:
        steps = jnp.exp(jax.random.uniform(jax.random.fold_in(own, axis_at), (shards_of,), jnp.float32, least / len(shards), top_value / len(shards)))
        factor_of = factor_of * jnp.repeat(steps, dims[axis_at] // shards_of).reshape([-1 if axis == axis_at else 1 for axis in range(len(dims))])
    return factor_of


def rank_bounds(count, lean):
    portions = [(1 << 20) // math.isqrt(grade ** lean) + 1 for grade in range(1, count + 1)]
    scale = 1 + sum(portions) // (1 << 30)
    return np.cumsum(np.array([max(1, weight // scale) for weight in portions]))


def ranked_ids(key, shape, amount, slope):
    grid = rank_bounds(amount, slope)
    pick = jax.random.randint(jax.random.fold_in(key, 1), shape, 0, int(grid[amount - 1]))
    standing = jnp.searchsorted(jnp.asarray(grid, jnp.int32), pick, side="right")
    return jax.random.permutation(jax.random.fold_in(key, 2), amount)[standing].astype(jnp.int32)


def gaussian(stream_key, shape, scale, limit, shards=(), held_as=jnp.bfloat16):
    loudness = shard_levels(stream_key, shape, shards, -0.22, 0.18) if shards else 1.0
    result = jax.random.normal(stream_key, shape, jnp.float32) * scale * loudness
    return jnp.minimum(jnp.maximum(result, -limit), limit).astype(held_as)


def setup_inputs(seed: int = 0, part: int = 0) -> dict:
    keys = jax.random.split(jax.random.key(seed), 12)
    part_splits = jax.random.split(jax.random.fold_in(keys[11], part), 12)
    return {
        "hidden": draw_hidden(jax.random.fold_in(jax.random.fold_in(keys[11], part), 71), part),
        "skip": gaussian(part_splits[1], (REQUESTS, H, W, CHANNEL_COUNT), 1.0, 6.0, ((0, 2), (1, 8)), jnp.float32),
        "timestep_embedding_table": gaussian(keys[2], (STEPS, CHANNEL_COUNT), 1.0, 5.0, (), jnp.float32),
        "timesteps": draw_timesteps(jax.random.fold_in(jax.random.fold_in(keys[11], part), 71), part),
        "group_norm_gain": jnp.clip(1.0 + 0.18 * jax.random.normal(keys[4], (CHANNEL_COUNT,), jnp.float32), 0.1, 1.9),
        "group_norm_bias": gaussian(keys[5], (CHANNEL_COUNT,), 0.5, 3.0, (), jnp.float32),
        "kernel_weight": gaussian(keys[6], (9, CHANNEL_COUNT, CHANNEL_COUNT), (9 * CHANNEL_COUNT) ** -0.5, 0.0546875, ((1, 8), (2, 2))),
        "adapter_down_weight": gaussian(part_splits[7], (ADAPTER_COUNT, ADAPTER_RANK, 9 * CHANNEL_COUNT), (9 * CHANNEL_COUNT) ** -0.5, 0.0546875, ((0, 8),)),
        "adapter_up_weight": gaussian(part_splits[8], (ADAPTER_COUNT, ADAPTER_RANK, CHANNEL_COUNT), ADAPTER_RANK ** -0.5, 0.75, ((0, 8),)),
        "request_adapter": plant(ranked_ids(part_splits[9], (REQUESTS,), ADAPTER_COUNT, 2), jax.random.fold_in(part_splits[9], 3), 0, ADAPTER_COUNT - 1).astype(jnp.int32),
        "adapter_row_table": jax.random.permutation(part_splits[10], ADAPTER_COUNT).astype(jnp.int32),
    }


def make_taps(act):
    height, width, chans = act.shape
    padded = jnp.pad(act, ((1, 1), (1, 1), (0, 0)))
    pieces = [padded[dy:dy + height, dx:dx + width, :] for dy in range(3) for dx in range(3)]
    return jnp.stack(pieces, axis=2).reshape(height * width, 9 * chans)

def reference(hidden, skip, timestep_embedding_table, timesteps, group_norm_gain, group_norm_bias, kernel_weight, adapter_down_weight, adapter_up_weight, request_adapter, adapter_row_table):
    temb = jnp.take(timestep_embedding_table, timesteps, axis=0)
    shifted = hidden + temb[:, None, None, :]
    request_total, height, width, chans = shifted.shape
    grouped = shifted.reshape(request_total, height, width, GROUPS, chans // GROUPS)
    mean = lax.optimization_barrier(jnp.mean(grouped, axis=(1, 2, 4), keepdims=True))
    centered = grouped - mean
    var = lax.optimization_barrier(jnp.mean(centered * centered, axis=(1, 2, 4), keepdims=True))
    normed = (centered * lax.rsqrt(var + 1e-05)).reshape(request_total, height, width, chans)
    act = jax.nn.silu(normed * group_norm_gain + group_norm_bias).astype(jnp.bfloat16)
    weight = kernel_weight.reshape(9 * chans, chans)
    store_rows = jnp.take(adapter_row_table, request_adapter, axis=0).astype(jnp.int32)

    def single(items):
        one_act, resident_row = items
        taps = make_taps(one_act)
        base = jnp.dot(taps, weight, preferred_element_type=jnp.float32)
        down_factor = lax.dynamic_index_in_dim(adapter_down_weight, resident_row, 0, keepdims=False)
        upper_limit = lax.dynamic_index_in_dim(adapter_up_weight, resident_row, 0, keepdims=False)
        low = lax.dot_general(taps, down_factor, (((1,), (1,)), ((), ())), preferred_element_type=jnp.float32).astype(jnp.bfloat16)
        delta = jnp.dot(low, upper_limit, preferred_element_type=jnp.float32)
        return (base + delta).reshape(height, width, chans)
    conv = lax.map(single, (act, store_rows))
    return skip + conv
```

```python
import functools

import jax
import jax.numpy as jnp
from jax import lax
from jax.experimental import pallas as pl
from jax.experimental.pallas import tpu as pltpu
from jax.sharding import PartitionSpec as P

GROUPS = 32
LANES = 128
WIN = 256
MESH = pl.DeviceIdType.MESH
BF = jnp.bfloat16
F32 = jnp.float32


def hi_dot(a, b, dims):
    return lax.dot_general(
        a, b, (dims, ((), ())), precision=lax.Precision.HIGHEST, preferred_element_type=F32
    )


def block_kernel(
    n, own, reqs, width, chans,
    steps, asked, row_of, hid, table, gain, bias, w_hbm, d_hbm, u_hbm,
    out,
    rows, xin, taps, wpad, dall, uall, stat_out, stat_in, keep, zsend, zrecv,
    fsend, frecv, mine, lxs, lxr, lzs, lzr, lfs, lfr,
    st_s, st_r, wc_s, wc_r, wx_s, wx_r, w_l, d_s, d_r, d_l, dp_s, dp_r,
    ux_s, ux_r, u_l, uz_s, uz_r, up_s, up_r, a_s, a_r, xf_s, xf_r,
    z_s, z_r, lx_s, lx_r, lz_s, lz_r, lf_s, lf_r, f_s, f_r,
):
    me = lax.axis_index("patch")
    core = lax.axis_index("req")
    mate = 1 - core
    zs = n // 2
    z, x = me // 2, me % 2
    other = 1 - x
    near = me + 1 - 2 * x
    hub = core == x
    half = chans // 2
    cells = reqs * width
    per, rank, _ = d_hbm.shape
    hrank = rank // 2
    win = xin.shape[2]
    top = zs - 1
    temb = [table[pl.ds(steps[r], 1), :] for r in range(reqs)]
    sel = [row_of[asked[r]] for r in range(reqs)]

    barrier = pltpu.get_barrier_semaphore()
    for k in range(1, n):
        pl.semaphore_signal(barrier, inc=1, device_id={"patch": (me + k) % n}, device_id_type=MESH)
    pl.semaphore_signal(barrier, inc=1, device_id={"req": mate}, device_id_type=MESH)
    pl.semaphore_wait(barrier, n)

    def remote(src, dst, send, recv, to):
        return pltpu.make_async_remote_copy(
            src_ref=src, dst_ref=dst, send_sem=send, recv_sem=recv, device_id=to, device_id_type=MESH
        )

    side, twin = {"patch": near}, {"req": mate}

    inner = pl.multiple_of((z % 2) * (win - 2 * own), 32)

    def w_dst(t, j):
        at = pl.multiple_of((t % 3) * win + inner + j * own, 32)
        return wpad.at[t // 3, pl.ds(at, own), :]

    def w_local(t):
        return pltpu.make_async_copy(w_hbm.at[t], w_dst(t, x), w_l.at[t])

    def w_twin(t):
        return remote(w_hbm.at[t], w_dst(t, x), wc_s.at[0, t], wc_r.at[0, t], twin)

    def w_side(t):
        return remote(w_hbm.at[t], w_dst(t, x), wx_s.at[t], wx_r.at[t], side)

    def w_pass(t):
        return remote(w_dst(t, other), w_dst(t, other), wc_s.at[1, t], wc_r.at[1, t], twin)

    rank_at = pl.multiple_of(core * hrank, hrank)

    def u_src(c):
        return u_hbm.at[:, pl.ds(rank_at, hrank), pl.ds(pl.multiple_of(c * half, LANES), half)]

    def u_dst(at, count):
        return uall.at[pl.ds(at, count), pl.ds(rank_at, hrank), :]

    u_own = pltpu.make_async_copy(u_src(x), u_dst(me * per, per), u_l)
    u_side = remote(u_src(other), u_dst(me * per, per), ux_s, ux_r, side)

    def u_col(peer, src):
        block = u_dst(src * 2 * per, 2 * per)
        return remote(block, block, uz_s.at[peer], uz_r.at[src], {"patch": peer * 2 + x})

    def d_src(a, t):
        return d_hbm.at[a, :, pl.ds(pl.multiple_of(t * chans, LANES), chans)]

    def d_dst(j, a, t):
        return dall.at[j * per + a, t % 3, pl.ds(pl.multiple_of((t // 3) * rank, rank), rank), :]

    def d_own(a, t):
        return pltpu.make_async_copy(d_src(a, t), d_dst(x, a, t), d_l.at[a, t])

    def d_side(t):
        return remote(d_src(core, t), d_dst(x, core, t), d_s.at[t], d_r.at[t], side)

    def d_pass(a):
        part = dall.at[other * per + a]
        return remote(part, part, dp_s, dp_r, twin)

    @pl.loop(0, 9)
    def _(t):
        @pl.when(hub)
        def _():
            w_local(t).start()
            w_twin(t).start()

        @pl.when(jnp.logical_not(hub))
        def _():
            w_side(t).start()

    u_own.start()
    u_side.start()
    for a in range(per):
        @pl.loop(0, 9)
        def _(t, a=a):
            d_own(a, t).start()

    spare = pl.multiple_of((1 - z % 2) * 2 * own, 32)
    for t in range(9):
        wpad[t // 3, pl.ds(t % 3 * win + spare, win - 2 * own), :] = jnp.zeros((win - 2 * own, half), BF)

    c_of = lax.broadcasted_iota(jnp.int32, (chans, LANES), 0)
    g_of = lax.broadcasted_iota(jnp.int32, (chans, LANES), 1)
    size = chans // GROUPS
    member = jnp.where((c_of >= g_of * size) & (c_of < (g_of + 1) * size), 1.0, 0.0).astype(F32)
    count = width * size
    sums = [
        jnp.sum(hid[r * width : (r + 1) * width, :] + temb[r], axis=0, keepdims=True)
        for r in range(reqs)
    ]
    pad = [jnp.zeros((8 - reqs, chans), F32)] if reqs < 8 else []
    mean = hi_dot(jnp.concatenate(sums + pad, axis=0), member, ((1,), (0,))) / count
    wide = hi_dot(mean, member, ((1,), (1,)))
    squares = []
    for r in range(reqs):
        c = hid[r * width : (r + 1) * width, :] + temb[r] - wide[r : r + 1, :]
        squares.append(jnp.sum(c * c, axis=0, keepdims=True))
    second = hi_dot(jnp.concatenate(squares + pad, axis=0), member, ((1,), (0,)))
    stat_out[0] = mean
    stat_out[1] = second

    def st_copy(peer, src):
        return remote(stat_out, stat_in.at[src], st_s.at[peer], st_r.at[src], {"patch": peer})

    for k in range(1, n):
        st_copy((me + k) % n, me).start()
    stat_in[me] = stat_out[...]
    u_own.wait()
    u_side.wait_recv()
    for k in range(1, zs):
        u_col((z + k) % zs, z).start()
    for k in range(1, n):
        st_copy((me + k) % n, (me + k) % n).wait_recv()
    means = stat_in[:, 0]
    total_mean = jnp.sum(means, axis=0) / n
    spread = means - total_mean[None]
    var = (jnp.sum(stat_in[:, 1], axis=0) + count * jnp.sum(spread * spread, axis=0)) / (count * n)
    mean_w = hi_dot(total_mean, member, ((1,), (1,)))
    inv_w = hi_dot(lax.rsqrt(var + 1e-05), member, ((1,), (1,)))
    scale = gain[...].reshape(1, chans)
    shift = bias[...].reshape(1, chans)
    for r in range(reqs):
        at = slice(r * width, (r + 1) * width)
        v = (hid[at, :] + temb[r] - mean_w[r : r + 1, :]) * inv_w[r : r + 1, :]
        v = v * scale + shift
        v = (v / (1.0 + jnp.exp(-v))).astype(BF)
        rows[z, 0, at, :] = v[:, :half]
        rows[z, 1, at, :] = v[:, half:]

    def a_copy(way, s, h):
        to = {"patch": me + 2 - 4 * way}
        return remote(rows.at[s, h], rows.at[s, h], a_s.at[way, s, h], a_r.at[s, h], to)

    def own_half(second):
        @pl.when(z < top)
        def _():
            a_copy(0, z, 1 - second).start()

        @pl.when(z > 0)
        def _():
            a_copy(1, z, second).start()

    slot = z // 2
    lane = pl.multiple_of((z % 2) * (half - win), LANES)

    def x_fwd(s):
        return remote(rows.at[s, slot, :, pl.ds(lane, win)], xin.at[s], xf_s.at[s], xf_r.at[s], side)

    px = lax.broadcasted_iota(jnp.int32, (cells, win), 0) % width

    def lay(y, v):
        v = v.astype(F32)
        taps[y + 1, :, 0:win] = jnp.where(px == 0, 0.0, pltpu.roll(v, 1, 0)).astype(BF)
        taps[y + 1, :, win : 2 * win] = v.astype(BF)
        taps[y + 1, :, 2 * win :] = jnp.where(px == width - 1, 0.0, pltpu.roll(v, cells - 1, 0)).astype(BF)

    def got(s):
        x_fwd(s).start()
        lay(2 * s + x, rows[s, slot, :, pl.ds(lane, win)])

    def hop(k, second):
        lo, hi = 1 - second, second

        @pl.when(z >= k)
        def _():
            a_copy(0, z - k, lo).wait_recv()

            @pl.when(z < top)
            def _():
                a_copy(0, z - k, lo).start()

        @pl.when(z + k <= top)
        def _():
            a_copy(1, z + k, hi).wait_recv()

            @pl.when(z > 0)
            def _():
                a_copy(1, z + k, hi).start()

    def take(k, second):
        lo, hi = 1 - second, second

        @pl.when(jnp.logical_and(z >= k, slot == lo))
        def _():
            got(z - k)

        @pl.when(jnp.logical_and(z + k <= top, slot == hi))
        def _():
            got(z + k)

    own_half(0)
    got(z)
    taps[0] = jnp.zeros(taps.shape[1:], BF)
    taps[n + 1] = jnp.zeros(taps.shape[1:], BF)
    hop(1, 0)
    own_half(1)
    take(1, 0)
    hop(2, 0)
    take(2, 0)
    hop(3, 0)
    take(3, 0)
    hop(1, 1)
    take(1, 1)

    @pl.loop(0, 9)
    def _(t):
        d_side(t).start()

    @pl.when(hub)
    def _():
        @pl.loop(0, 9)
        def _(t):
            w_side(t).wait_recv()
            w_pass(t).start()

    @pl.loop(0, zs)
    def _(s):
        x_fwd(s).wait_recv()
        lay(2 * s + other, xin[s])

    @pl.when(hub)
    def _():
        @pl.loop(0, 9)
        def _(t):
            w_local(t).wait()

    @pl.when(jnp.logical_not(hub))
    def _():
        @pl.loop(0, 9)
        def _(t):
            w_twin(t).wait_recv()
            w_pass(t).wait_recv()

    order = (3 * (1 - z // 2), (2 + 3 * z) % 5, 1 + z % 2, z)

    def conv(dest):
        for lo in range(0, half, WIN):
            hi = min(lo + WIN, half)
            s = jnp.zeros((2 * cells, hi - lo), F32)
            for dy in range(3):
                lhs = taps[pl.ds(2 * dest + dy, 2)].reshape(2 * cells, 3 * win)
                s += jnp.dot(lhs, wpad[dy, :, lo:hi], preferred_element_type=F32)
            keep[dest, :, :, lo:hi] = s.reshape(2, cells, hi - lo)

    def z_copy(dest, a):
        after = jnp.where(dest > z, z + 1, z - 1)
        at = jnp.where(jnp.logical_and(dest < z, after == dest), zs, dest)
        return remote(
            zsend.at[dest, a], zrecv.at[at, a], z_s.at[dest, a], z_r.at[at, a], {"patch": after * 2 + x}
        )

    def z_arrival(at, a):
        return pltpu.make_async_copy(zrecv.at[at, a], zrecv.at[at, a], z_r.at[at, a])

    def push(dest):
        for a in (other, x):
            upward = jnp.logical_and(dest > z, z > 0)
            downward = jnp.logical_and(dest < z, z < top)

            @pl.when(jnp.logical_or(upward, downward))
            def _(a=a):
                z_arrival(dest, a).wait()
                keep[dest, a] += zrecv[dest, a].astype(F32)

            zsend[dest, a] = keep[dest, a].astype(BF)
            z_copy(dest, a).start()

    end = jnp.logical_or(z == 0, z == top)
    for i in range(zs):
        conv(order[i])
        if i < zs - 1:
            @pl.when(end)
            def _(i=i):
                push(order[i])
        if i == 0:
            hop(2, 1)
    for i in range(zs - 1):
        @pl.when(jnp.logical_not(end))
        def _(i=i):
            push(order[i])
    hop(3, 1)

    @pl.loop(0, 9)
    def _(t):
        d_side(t).wait_recv()

    d_pass(core).start()
    for a in range(per):
        @pl.loop(0, 9)
        def _(t, a=a):
            d_own(a, t).wait()

    for k in range(1, zs):
        src = (z + k) % zs
        u_col(src, src).wait_recv()

    def u_twin(at):
        part = uall.at[:, pl.ds(pl.multiple_of(at * hrank, hrank), hrank), :]
        return remote(part, part, up_s, up_r, twin)

    u_twin(core).start()
    d_pass(mate).wait_recv()

    pq = lax.broadcasted_iota(jnp.int32, (zs * width, 3 * rank), 0) % width
    for q in range(reqs // 2):
        pair_mine, pair_side = [], []
        for r in (2 * q, 2 * q + 1):
            stored = sel[r] - z * 2 * per
            here = jnp.logical_and(stored >= 0, stored < 2 * per)
            index = jnp.clip(stored, 0, 2 * per - 1)
            prod = []
            for dx in range(3):
                p = jnp.zeros((zs * width, 3 * rank), F32)
                for h in range(2):
                    lhs = rows[:, h, r * width : (r + 1) * width, :].reshape(zs * width, half)
                    p += lax.dot_general(
                        lhs, dall[index, dx, :, h * half : (h + 1) * half], (((1,), (1,)), ((), ())),
                        preferred_element_type=F32,
                    )
                prod.append(p)
            s = prod[1]
            s += jnp.where(pq == 0, 0.0, pltpu.roll(prod[0], 1, 0))
            s += jnp.where(pq == width - 1, 0.0, pltpu.roll(prod[2], zs * width - 1, 0))
            s = jnp.where(here, s, 0.0).reshape(zs, width, 3 * rank)
            above, level, below = s[:, :, :rank], s[:, :, rank : 2 * rank], s[:, :, 2 * rank :]
            none = jnp.zeros((1, width, rank), F32)
            even = above + jnp.concatenate([below[1:], none], axis=0)
            odd = jnp.concatenate([none, above[:-1]], axis=0) + below
            pair_mine.append(level)
            pair_side.append(jnp.where(x == 0, even, odd))
        at = slice(q * width, (q + 1) * width)
        mine[:, at, :] = jnp.concatenate(pair_mine, axis=2)
        lxs[:, at, :] = jnp.concatenate(pair_side, axis=2).astype(BF)

    lx_copy = remote(lxs, lxr, lx_s, lx_r, side)
    lx_copy.start()

    def lz_copy(peer, src):
        return remote(lzs.at[peer], lzr.at[src], lz_s.at[peer], lz_r.at[src], {"patch": peer * 2 + x})

    lx_copy.wait_recv()
    lzs[...] = (mine[...] + lxr[...].astype(F32)).astype(BF)
    for k in range(1, zs):
        lz_copy((z + k) % zs, z).start()
    both = mine[z] + lxr[z].astype(F32)
    for k in range(1, zs):
        src = (z + k) % zs
        lz_copy(src, src).wait_recv()
        both += lzr[src].astype(F32)
    lfs[...] = both.astype(BF)
    lf_copy = remote(lfs, lfr, lf_s, lf_r, side)
    lf_copy.start()
    u_twin(mate).wait_recv()
    lf_copy.wait_recv()

    def f_copy():
        return remote(fsend, frecv, f_s, f_r, side)

    for a, src in ((other, lfr), (x, lfs)):
        for r in range(reqs):
            low = src[r // 2 * width : (r // 2 + 1) * width, r % 2 * rank : (r % 2 + 1) * rank]
            at = slice(r * width, (r + 1) * width)
            keep[z, a, at, :] += jnp.dot(low, uall[sel[r]], preferred_element_type=F32)

        @pl.when(z > 0)
        def _(a=a):
            z_arrival(z, a).wait()
            keep[z, a] += zrecv[z, a].astype(F32)

        @pl.when(z < top)
        def _(a=a):
            z_arrival(zs, a).wait()
            keep[z, a] += zrecv[zs, a].astype(F32)

        if src is lfr:
            fsend[...] = keep[z, other].astype(BF)
            f_copy().start()

    out[:, pl.ds(pl.multiple_of(x * half, LANES), half)] = keep[z, x]
    f_copy().wait_recv()
    out[:, pl.ds(pl.multiple_of(other * half, LANES), half)] = frecv[...].astype(F32)

    f_copy().wait_send()
    lf_copy.wait_send()
    lx_copy.wait_send()
    d_pass(core).wait_send()
    u_twin(core).wait_send()
    u_side.wait_send()
    for k in range(1, zs):
        u_col((z + k) % zs, z).wait_send()
        lz_copy((z + k) % zs, z).wait_send()
    for k in range(1, n):
        st_copy((me + k) % n, me).wait_send()

    @pl.loop(0, 9)
    def _(t):
        d_side(t).wait_send()

        @pl.when(hub)
        def _():
            w_twin(t).wait_send()
            w_pass(t).wait_send()

        @pl.when(jnp.logical_not(hub))
        def _():
            w_side(t).wait_send()

    @pl.loop(0, zs)
    def _(s):
        x_fwd(s).wait_send()
        for h in range(2):
            @pl.when(jnp.logical_and(s <= z, z < top))
            def _(h=h):
                a_copy(0, s, h).wait_send()

            @pl.when(jnp.logical_and(s >= z, z > 0))
            def _(h=h):
                a_copy(1, s, h).wait_send()

        @pl.when(s != z)
        def _():
            for a in range(2):
                z_copy(s, a).wait_send()


def run_block(n, steps, asked, row_of, hid, table, gain, bias, weight, down, up):
    cells, chans = hid.shape
    reqs = asked.shape[0]
    width = cells // reqs
    own = weight.shape[1]
    per, rank, _ = down.shape
    zs = n // 2
    half = chans // 2
    win = -(-2 * own // LANES) * LANES
    dma = pltpu.SemaphoreType.DMA
    vmem = pl.BlockSpec(memory_space=pltpu.VMEM)
    hbm = pl.BlockSpec(memory_space=pl.ANY)
    smem = pl.BlockSpec(memory_space=pltpu.SMEM)
    low = (cells // 2, 2 * rank)
    return pl.pallas_call(
        functools.partial(block_kernel, n, own, reqs, width, chans),
        out_shape=jax.ShapeDtypeStruct((cells, chans), F32),
        in_specs=[smem] * 3 + [vmem] * 4 + [hbm] * 3,
        out_specs=vmem,
        scratch_shapes=[
            pltpu.VMEM((zs, 2, cells, half), BF),
            pltpu.VMEM((zs, cells, win), BF),
            pltpu.VMEM((n + 2, cells, 3 * win), BF),
            pltpu.VMEM((3, 3 * win, half), BF),
            pltpu.VMEM((2 * per, 3, 3 * rank, chans), BF),
            pltpu.VMEM((n * per, rank, half), BF),
            pltpu.VMEM((2, 8, LANES), F32),
            pltpu.VMEM((n, 2, 8, LANES), F32),
            pltpu.VMEM((zs, 2, cells, half), F32),
            pltpu.VMEM((zs, 2, cells, half), BF),
            pltpu.VMEM((zs + 1, 2, cells, half), BF),
            pltpu.VMEM((cells, half), BF),
            pltpu.VMEM((cells, half), BF),
            pltpu.VMEM((zs,) + low, F32),
            pltpu.VMEM((zs,) + low, BF),
            pltpu.VMEM((zs,) + low, BF),
            pltpu.VMEM((zs,) + low, BF),
            pltpu.VMEM((zs,) + low, BF),
            pltpu.VMEM(low, BF),
            pltpu.VMEM(low, BF),
            dma((n,)), dma((n,)),
            dma((2, 9)), dma((2, 9)), dma((9,)), dma((9,)), dma((9,)),
            dma((9,)), dma((9,)), dma((per, 9)), dma, dma,
            dma, dma, dma, dma((zs,)), dma((zs,)), dma, dma,
            dma((2, zs, 2)), dma((zs, 2)), dma((zs,)), dma((zs,)),
            dma((zs, 2)), dma((zs + 1, 2)),
            dma, dma, dma((zs,)), dma((zs,)), dma, dma, dma, dma,
        ],
        compiler_params=pltpu.CompilerParams(
            collective_id=0, has_side_effects=True, vmem_limit_bytes=56 * 2**20
        ),
        cost_estimate=pl.CostEstimate(
            flops=2 * n * cells * 9 * win * half, bytes_accessed=10**8, transcendentals=0
        ),
    )(steps, asked, row_of, hid, table, gain, bias, weight, down, up)


def split_contraction(
    hidden, skip, timestep_embedding_table, timesteps, group_norm_gain, group_norm_bias,
    kernel_weight, adapter_down_weight, adapter_up_weight, request_adapter, adapter_row_table,
):
    shape = hidden.shape
    flat = (shape[0] * shape[1] * shape[2], shape[3])
    total = run_block(
        lax.axis_size("patch"), timesteps, request_adapter, adapter_row_table,
        hidden.reshape(flat), timestep_embedding_table, group_norm_gain, group_norm_bias,
        kernel_weight, adapter_down_weight, adapter_up_weight,
    )
    return skip + total.reshape(shape)


def fits(n, hidden, kernel_weight, down):
    own = kernel_weight.shape[1]
    return (
        n == 8 and hidden.shape[1] == 1 and hidden.shape[0] in (2, 4, 6, 8)
        and hidden.shape[3] == 1280 and own == 160 and down.shape[:2] == (2, 64)
    )


def broadcast(block, axis, owner):
    block = jnp.where(lax.axis_index(axis) == owner, block, jnp.zeros_like(block))
    return lax.psum(block, axis)


def padded(cells, sides, width):
    for axis, dim in sides:
        count = lax.axis_size(axis)
        ends = count - 1
        head = lax.slice_in_dim(cells, 0, width, axis=dim)
        tail = lax.slice_in_dim(cells, cells.shape[dim] - width, cells.shape[dim], axis=dim)
        cells = jnp.concatenate(
            [
                lax.ppermute(tail, axis, [(i, (i + 1) % count) for i in range(ends)]),
                cells,
                lax.ppermute(head, axis, [((i + 1) % count, i) for i in range(ends)]),
            ],
            axis=dim,
        )
    return cells


def from_partner(x, axis, stride):
    return lax.ppermute(x, axis, [(i, i ^ 1 << stride) for i in range(lax.axis_size(axis))])


def make_taps(extended, rows, width):
    pieces = [extended[:, dy : dy + rows, dx : dx + width, :] for dy in range(3) for dx in range(3)]
    stacked = jnp.stack(pieces, axis=3)
    count = stacked.shape[0] * rows * width
    return stacked.reshape(count, 9, stacked.shape[-1])


def load_adapter_factors(
    adapter_down_weight, adapter_up_weight, request_adapter, adapter_row_table, request_total
):
    resident_count = adapter_down_weight.shape[0]
    fetched = []
    for request in range(request_total):
        resident_row = adapter_row_table[request_adapter[request]]
        owner = resident_row // resident_count
        store_position = resident_row % resident_count
        resident_down = lax.dynamic_index_in_dim(
            adapter_down_weight, store_position, 0, keepdims=False
        )
        resident_up = lax.dynamic_index_in_dim(adapter_up_weight, store_position, 0, keepdims=False)
        fetched.append(
            (broadcast(resident_down, "patch", owner), broadcast(resident_up, "patch", owner))
        )
    return fetched


def shards(
    hidden,
    skip,
    timestep_embedding_table,
    timesteps,
    group_norm_gain,
    group_norm_bias,
    kernel_weight,
    adapter_down_weight,
    adapter_up_weight,
    request_adapter,
    adapter_row_table,
):
    request_total, rows, width, chans = hidden.shape
    steps_count = timestep_embedding_table.shape[0]
    onehot = (timesteps[:, None] == jnp.arange(steps_count, dtype=jnp.int32)[None, :]).astype(
        jnp.float32
    )
    temb = jnp.dot(
        onehot,
        timestep_embedding_table,
        preferred_element_type=jnp.float32,
        precision=lax.Precision.HIGHEST,
    )
    shifted = hidden + temb[:, None, None, :]
    grouped = shifted.reshape(request_total, rows, width, GROUPS, chans // GROUPS)
    count = rows * lax.axis_size("patch") * width * (chans // GROUPS)
    totals = lax.psum(jnp.sum(grouped, axis=(1, 2, 4)), "patch")
    mean = totals / count
    centered = grouped - mean[:, None, None, :, None]
    squares = lax.psum(jnp.sum(centered * centered, axis=(1, 2, 4)), "patch")
    var = squares / count
    normed = (centered * lax.rsqrt(var + 1e-05)[:, None, None, :, None]).reshape(
        request_total, rows, width, chans
    )
    act = jax.nn.silu(normed * group_norm_gain + group_norm_bias).astype(jnp.bfloat16)
    extended = padded(act, (("patch", 1),), 1)
    extended = jnp.pad(extended, ((0, 0), (0, 0), (1, 1), (0, 0)))
    partner = from_partner(extended, "req", 0)
    taps = make_taps(jnp.concatenate([extended, partner], axis=0), rows, width)
    pixels = request_total * rows * width
    conv_half = jnp.einsum(
        "ptc,tco->po",
        taps,
        lax.all_gather(kernel_weight, "patch", axis=1, tiled=True),
        preferred_element_type=jnp.float32,
    )
    own_half = conv_half[:pixels]
    returned = from_partner(conv_half[pixels:], "req", 0)
    first = lax.axis_index("req") == 0
    left_half = jnp.where(first, own_half, returned)
    right_half = jnp.where(first, returned, own_half)
    conv = jnp.concatenate([left_half, right_half], axis=1).reshape(
        request_total, rows * width, chans
    )
    own_taps = taps[:pixels].reshape(request_total, rows * width, 9 * chans)
    adapter_factors = load_adapter_factors(
        adapter_down_weight, adapter_up_weight, request_adapter, adapter_row_table, request_total
    )
    deltas = []
    for request in range(request_total):
        down_factor, upper_limit = adapter_factors[request]
        low = lax.dot_general(
            own_taps[request],
            down_factor,
            (((1,), (1,)), ((), ())),
            preferred_element_type=jnp.float32,
        ).astype(jnp.bfloat16)
        deltas.append(jnp.dot(low, upper_limit, preferred_element_type=jnp.float32))
    total = conv + jnp.stack(deltas, axis=0)
    return skip + total.reshape(request_total, rows, width, chans)


def solution(mesh):
    def step(*args):
        n = lax.axis_size("patch")
        if fits(n, args[0], args[6], args[7]):
            return split_contraction(*args)
        return shards(*args)

    return jax.shard_map(
        step,
        mesh=mesh,
        in_specs=(
            P(("groups", "req"), "patch", None, None),
            P(("groups", "req"), "patch", None, None),
            P(),
            P(("groups", "req")),
            P(),
            P(),
            P(None, "patch", "req"),
            P(("groups", "patch"), None, None),
            P(("groups", "patch"), None, None),
            P(("groups", "req")),
            P("groups"),
        ),
        out_specs=P(("groups", "req"), "patch", None, None),
        check_vma=False,
    )
```

```python
import functools

import jax
import jax.numpy as jnp
from jax import lax
from jax.experimental import pallas as pl
from jax.experimental.pallas import tpu as pltpu
from jax.sharding import PartitionSpec as P

GROUPS = 32
LANES = 128
WIN = 256
MESH = pl.DeviceIdType.MESH
BF = jnp.bfloat16
F32 = jnp.float32


def hi_dot(a, b, dims):
    return lax.dot_general(
        a, b, (dims, ((), ())), precision=lax.Precision.HIGHEST, preferred_element_type=F32
    )


def block_kernel(
    n, own, reqs, width, chans,
    steps, asked, row_of, hid, table, gain, bias, w_hbm, d_hbm, u_hbm,
    out,
    rows, xin, taps, wpad, dall, uall, stat_out, stat_in, keep, zsend, zrecv,
    fsend, frecv, mine, lxs, lxr, lzs, lzr, lows,
    st_s, st_r, wc_s, wc_r, wx_s, wx_r, wy_s, wy_r, w_l, d_s, d_r, d_l, dp_s, dp_r,
    ux_s, ux_r, u_l, uz_s, uz_r, up_s, up_r, a_s, a_r, xf_s, xf_r,
    z_s, z_r, lx_s, lx_r, lz_s, lz_r, f_s, f_r,
):
    me = lax.axis_index("patch")
    core = lax.axis_index("req")
    mate = 1 - core
    zs = n // 2
    z, x = me // 2, me % 2
    other = 1 - x
    near = me + 1 - 2 * x
    hub = core == x
    half = chans // 2
    cells = reqs * width
    per, rank, _ = d_hbm.shape
    hrank = rank // 2
    win = xin.shape[2]
    top = zs - 1
    temb = [table[pl.ds(steps[r], 1), :] for r in range(reqs)]
    sel = [row_of[asked[r]] for r in range(reqs)]

    barrier = pltpu.get_barrier_semaphore()
    for k in range(1, n):
        pl.semaphore_signal(barrier, inc=1, device_id={"patch": (me + k) % n}, device_id_type=MESH)
    part = lax.axis_index("groups")
    for to in ({"req": mate}, {"groups": 1 - part}):
        pl.semaphore_signal(barrier, inc=1, device_id=to, device_id_type=MESH)
    pl.semaphore_wait(barrier, n + 1)

    def remote(src, dst, send, recv, to):
        return pltpu.make_async_remote_copy(
            src_ref=src, dst_ref=dst, send_sem=send, recv_sem=recv, device_id=to, device_id_type=MESH
        )

    side, twin, peer_part = {"patch": near}, {"req": mate}, {"groups": 1 - part}

    inner = pl.multiple_of((z % 2) * (win - 2 * own), 32)

    cut = own // 2

    def w_src(t, lo, size):
        return w_hbm.at[t, :, pl.ds(lo, size), :]

    def w_dst(t, j, lo, size):
        return wpad.at[t, :, pl.ds(pl.multiple_of(inner + j * own + lo, 16), size), :]

    def w_local(t):
        return pltpu.make_async_copy(w_src(t, 0, own), w_dst(t, x, 0, own), w_l.at[t])

    def w_twin(t):
        return remote(w_src(t, 0, own), w_dst(t, x, 0, own), wc_s.at[0, t], wc_r.at[0, t], twin)

    def w_side(t):
        lo = pl.multiple_of(part * cut, 16)
        return remote(w_src(t, lo, cut), w_dst(t, x, lo, cut), wx_s.at[t], wx_r.at[t], side)

    def w_part(t, from_part):
        block = w_dst(t, other, pl.multiple_of(from_part * cut, 16), cut)
        return remote(block, block, wy_s.at[t], wy_r.at[t], peer_part)

    def w_pass(t, from_part):
        block = w_dst(t, other, pl.multiple_of(from_part * cut, 16), cut)
        return remote(block, block, wc_s.at[1 + from_part, t], wc_r.at[1 + from_part, t], twin)

    rank_at = pl.multiple_of(core * hrank, hrank)

    def u_src(c):
        return u_hbm.at[:, pl.ds(rank_at, hrank), pl.ds(pl.multiple_of(c * half, LANES), half)]

    def u_dst(at, count):
        return uall.at[pl.ds(at, count), pl.ds(rank_at, hrank), :]

    u_own = pltpu.make_async_copy(u_src(x), u_dst(me * per, per), u_l)
    u_side = remote(u_src(other), u_dst(me * per, per), ux_s, ux_r, side)

    def u_col(way, src):
        block = u_dst(src * 2 * per, 2 * per)
        return remote(block, block, uz_s.at[way, src], uz_r.at[src], {"patch": me + 2 - 4 * way})

    def u_hop(k):
        @pl.when(z >= k)
        def _():
            u_col(0, z - k).wait_recv()

            @pl.when(z < top)
            def _():
                u_col(0, z - k).start()

        @pl.when(z + k <= top)
        def _():
            u_col(1, z + k).wait_recv()

            @pl.when(z > 0)
            def _():
                u_col(1, z + k).start()

    def d_src(a, t):
        return d_hbm.at[a, :, pl.ds(pl.multiple_of(t * chans, LANES), chans)]

    def d_dst(j, a, t):
        return dall.at[j * per + a, t % 3, pl.ds(pl.multiple_of((t // 3) * rank, rank), rank), :]

    def d_own(a, t):
        return pltpu.make_async_copy(d_src(a, t), d_dst(x, a, t), d_l.at[a, t])

    def d_side(t):
        return remote(d_src(core, t), d_dst(x, core, t), d_s.at[t], d_r.at[t], side)

    def d_pass(a):
        part = dall.at[other * per + a]
        return remote(part, part, dp_s, dp_r, twin)

    u_own.start()
    u_side.start()

    @pl.when(hub)
    def _():
        for t in range(3):
            w_local(t).start()
            w_twin(t).start()

    @pl.when(jnp.logical_not(hub))
    def _():
        for t in range(3):
            w_side(t).start()

    for a in range(per):
        @pl.loop(0, 9)
        def _(t, a=a):
            d_own(a, t).start()

    spare = pl.multiple_of((1 - z % 2) * 2 * own, 32)
    wpad[:, :, pl.ds(spare, win - 2 * own), :] = jnp.zeros((3, 3, win - 2 * own, half), BF)

    c_of = lax.broadcasted_iota(jnp.int32, (chans, LANES), 0)
    g_of = lax.broadcasted_iota(jnp.int32, (chans, LANES), 1)
    size = chans // GROUPS
    member = jnp.where((c_of >= g_of * size) & (c_of < (g_of + 1) * size), 1.0, 0.0).astype(F32)
    count = width * size
    sums = [
        jnp.sum(hid[r * width : (r + 1) * width, :] + temb[r], axis=0, keepdims=True)
        for r in range(reqs)
    ]
    pad = [jnp.zeros((8 - reqs, chans), F32)] if reqs < 8 else []
    mean = hi_dot(jnp.concatenate(sums + pad, axis=0), member, ((1,), (0,))) / count
    wide = hi_dot(mean, member, ((1,), (1,)))
    squares = []
    for r in range(reqs):
        c = hid[r * width : (r + 1) * width, :] + temb[r] - wide[r : r + 1, :]
        squares.append(jnp.sum(c * c, axis=0, keepdims=True))
    second = hi_dot(jnp.concatenate(squares + pad, axis=0), member, ((1,), (0,)))
    stat_out[0] = mean
    stat_out[1] = second

    def st_copy(peer, src):
        return remote(stat_out, stat_in.at[src], st_s.at[peer], st_r.at[src], {"patch": peer})

    for k in range(1, n):
        st_copy((me + k) % n, me).start()
    stat_in[me] = stat_out[...]
    u_own.wait()
    u_side.wait_recv()

    @pl.when(z < top)
    def _():
        u_col(0, z).start()

    @pl.when(z > 0)
    def _():
        u_col(1, z).start()

    for k in range(1, n):
        st_copy((me + k) % n, (me + k) % n).wait_recv()
    means = stat_in[:, 0]
    total_mean = jnp.sum(means, axis=0) / n
    spread = means - total_mean[None]
    var = (jnp.sum(stat_in[:, 1], axis=0) + count * jnp.sum(spread * spread, axis=0)) / (count * n)
    mean_w = hi_dot(total_mean, member, ((1,), (1,)))
    inv_w = hi_dot(lax.rsqrt(var + 1e-05), member, ((1,), (1,)))
    scale = gain[...].reshape(1, chans)
    shift = bias[...].reshape(1, chans)
    for r in range(reqs):
        at = slice(r * width, (r + 1) * width)
        v = (hid[at, :] + temb[r] - mean_w[r : r + 1, :]) * inv_w[r : r + 1, :]
        v = v * scale + shift
        rows[z, at, :] = (v / (1.0 + jnp.exp(-v))).astype(BF)

    spans = (
        ((chans - win, win), (half, half - win), (0, half)),
        ((0, win), (win, half - win), (half, half)),
    )

    def a_copy(way, s, m):
        block = rows.at[s, :, pl.ds(*spans[way][m])]
        to = {"patch": me + 2 - 4 * way}
        return remote(block, block, a_s.at[way, s, m], a_r.at[s, m], to)

    def back(way, k):
        return z + k if way else z - k

    def hop(way, k, m):
        a_copy(way, back(way, k), m).wait_recv()

        @pl.when(middle)
        def _():
            a_copy(way, back(way, k), m).start()

    lane = pl.multiple_of(z * 2 * own // LANES * LANES, LANES)

    def x_fwd(s):
        return remote(rows.at[s, :, pl.ds(lane, win)], xin.at[s], xf_s.at[s], xf_r.at[s], side)

    px = lax.broadcasted_iota(jnp.int32, (cells, win), 0) % width

    def lay(y, v):
        v = v.astype(F32)
        taps[y + 1, :, 0:win] = jnp.where(px == 0, 0.0, pltpu.roll(v, 1, 0)).astype(BF)
        taps[y + 1, :, win : 2 * win] = v.astype(BF)
        taps[y + 1, :, 2 * win :] = jnp.where(px == width - 1, 0.0, pltpu.roll(v, cells - 1, 0)).astype(BF)

    def got(s):
        x_fwd(s).start()
        lay(2 * s + x, rows[s, :, pl.ds(lane, win)])

    def share_weights():
        @pl.when(hub)
        def _():
            for t in range(3):
                w_side(t).wait_recv()
                w_part(t, part).start()
                w_pass(t, part).start()

    def send_down(lo, hi):
        @pl.loop(lo, hi)
        def _(t):
            d_side(t).start()

    end = jnp.logical_or(z == 0, z == top)
    middle = jnp.logical_not(end)

    @pl.when(z < top)
    def _():
        a_copy(0, z, 0).start()

    @pl.when(z > 0)
    def _():
        a_copy(1, z, 0).start()

    got(z)
    taps[0] = jnp.zeros(taps.shape[1:], BF)
    taps[n + 1] = jnp.zeros(taps.shape[1:], BF)

    def at_end(way):
        for m in (1, 2):
            a_copy(1 - way, z, m).start()
        for k in range(1, zs):
            hop(way, k, 0)
            got(back(way, k))
            if k == 1:
                share_weights()
        send_down(0, 9)

    def at_middle(way):
        send_down(0, 3)
        hop(1 - way, 1, 0)
        hop(way, 1, 0)
        a_copy(way, z, 1).start()
        share_weights()
        hop(1 - way, 2, 0)
        a_copy(1 - way, z, 1).start()
        hop(way, 1, 1)
        for k in (1, 2):
            hop(1 - way, k, 1)
            got(back(1 - way, k))
        for to in (way, 1 - way):
            a_copy(to, z, 2).start()
        hop(way, 1, 2)
        got(back(way, 1))
        send_down(3, 9)

    for at, place, way in ((0, at_end, 1), (1, at_middle, 0), (2, at_middle, 1), (3, at_end, 0)):
        @pl.when(z == at)
        def _(place=place, way=way):
            place(way)

    @pl.when(hub)
    def _():
        for t in range(3):
            w_part(t, 1 - part).wait_recv()
            w_pass(t, 1 - part).start()

    @pl.loop(0, zs)
    def _(s):
        x_fwd(s).wait_recv()
        lay(2 * s + other, xin[s])

    @pl.when(hub)
    def _():
        for t in range(3):
            w_local(t).wait()

    @pl.when(jnp.logical_not(hub))
    def _():
        for t in range(3):
            w_twin(t).wait_recv()
            w_pass(t, 0).wait_recv()
            w_pass(t, 1).wait_recv()

    order = (3 * (1 - z // 2), (2 + 3 * z) % 5, 1 + z % 2, z)

    def conv(dest):
        for lo in range(0, half, WIN):
            hi = min(lo + WIN, half)
            s = jnp.zeros((2 * cells, hi - lo), F32)
            for dy in range(3):
                lhs = taps[pl.ds(2 * dest + dy, 2)].reshape(2 * cells, 3 * win)
                rhs = wpad[dy, :, :, lo:hi].reshape(3 * win, hi - lo)
                s += jnp.dot(lhs, rhs, preferred_element_type=F32)
            keep[dest, :, :, lo:hi] = s.reshape(2, cells, hi - lo)

    def z_copy(dest, a):
        after = jnp.where(dest > z, z + 1, z - 1)
        at = jnp.where(jnp.logical_and(dest < z, after == dest), zs, dest)
        return remote(
            zsend.at[dest, a], zrecv.at[at, a], z_s.at[dest, a], z_r.at[at, a], {"patch": after * 2 + x}
        )

    def z_arrival(at, a):
        return pltpu.make_async_copy(zrecv.at[at, a], zrecv.at[at, a], z_r.at[at, a])

    def push(dest, a):
        upward = jnp.logical_and(dest > z, z > 0)
        downward = jnp.logical_and(dest < z, z < top)

        @pl.when(jnp.logical_or(upward, downward))
        def _():
            z_arrival(dest, a).wait()
            keep[dest, a] += zrecv[dest, a].astype(F32)

        zsend[dest, a] = keep[dest, a].astype(BF)
        z_copy(dest, a).start()

    for i in range(zs):
        conv(order[i])
        if i < 2:
            for at, way in ((1, 1), (2, 0)):
                @pl.when(z == at)
                def _(i=i, way=way):
                    hop(way, i + 1, 2)

            @pl.when(middle)
            def _(i=i):
                u_hop(i + 1)
        if i < zs - 1:
            push(order[i], other)
            if i < zs - 2:
                push(order[i], x)
            else:
                @pl.when(middle)
                def _(i=i):
                    push(order[i], x)

    @pl.when(end)
    def _():
        u_hop(1)
        u_hop(2)

    for at, way in ((0, 1), (top, 0)):
        @pl.when(z == at)
        def _(way=way):
            for k in range(1, zs):
                for m in (1, 2):
                    a_copy(way, back(way, k), m).wait_recv()

    @pl.loop(0, 9)
    def _(t):
        d_side(t).wait_recv()

    d_pass(core).start()
    for a in range(per):
        @pl.loop(0, 9)
        def _(t, a=a):
            d_own(a, t).wait()

    u_hop(3)

    def u_twin(at):
        part = uall.at[:, pl.ds(pl.multiple_of(at * hrank, hrank), hrank), :]
        return remote(part, part, up_s, up_r, twin)

    u_twin(core).start()
    d_pass(mate).wait_recv()

    pq = lax.broadcasted_iota(jnp.int32, (zs * width, 3 * rank), 0) % width
    for q in range(reqs // 2):
        pair_mine, pair_side = [], []
        for r in (2 * q, 2 * q + 1):
            stored = sel[r] - z * 2 * per
            here = jnp.logical_and(stored >= 0, stored < 2 * per)
            index = jnp.clip(stored, 0, 2 * per - 1)
            prod = []
            for dx in range(3):
                lhs = rows[:, r * width : (r + 1) * width, :].reshape(zs * width, chans)
                prod.append(
                    lax.dot_general(
                        lhs, dall[index, dx], (((1,), (1,)), ((), ())), preferred_element_type=F32
                    )
                )
            s = prod[1]
            s += jnp.where(pq == 0, 0.0, pltpu.roll(prod[0], 1, 0))
            s += jnp.where(pq == width - 1, 0.0, pltpu.roll(prod[2], zs * width - 1, 0))
            s = jnp.where(here, s, 0.0).reshape(zs, width, 3 * rank)
            above, level, below = s[:, :, :rank], s[:, :, rank : 2 * rank], s[:, :, 2 * rank :]
            none = jnp.zeros((1, width, rank), F32)
            even = above + jnp.concatenate([below[1:], none], axis=0)
            odd = jnp.concatenate([none, above[:-1]], axis=0) + below
            pair_mine.append(level)
            pair_side.append(jnp.where(x == 0, even, odd))
        at = slice(q * width, (q + 1) * width)
        mine[:, at, :] = jnp.concatenate(pair_mine, axis=2)
        lxs[:, at, :] = jnp.concatenate(pair_side, axis=2).astype(BF)

    lx_copy = remote(lxs, lxr, lx_s, lx_r, side)
    lx_copy.start()

    def lz_copy(peer, src):
        return remote(lzs.at[peer // 2], lzr.at[src], lz_s.at[peer], lz_r.at[src], {"patch": peer})

    lx_copy.wait_recv()
    lzs[...] = (mine[...] + lxr[...].astype(F32)).astype(BF)
    for k in range(1, n):
        lz_copy((me + k) % n, me).start()

    @pl.when(end)
    def _():
        push(order[zs - 2], x)

    lzr[me] = lzs[z]
    for k in range(1, n):
        lz_copy((me + k) % n, (me + k) % n).wait_recv()
    for a in range(2):
        low = lzr[a].astype(F32)
        for k in range(1, zs):
            low += lzr[2 * k + a].astype(F32)
        lows[a] = low.astype(BF)
    u_twin(mate).wait_recv()

    def f_copy():
        return remote(fsend, frecv, f_s, f_r, side)

    for a in (other, x):
        for r in range(reqs):
            low = lows[a, r // 2 * width : (r // 2 + 1) * width, r % 2 * rank : (r % 2 + 1) * rank]
            at = slice(r * width, (r + 1) * width)
            keep[z, a, at, :] += jnp.dot(low, uall[sel[r]], preferred_element_type=F32)

        @pl.when(z > 0)
        def _(a=a):
            z_arrival(z, a).wait()
            keep[z, a] += zrecv[z, a].astype(F32)

        @pl.when(z < top)
        def _(a=a):
            z_arrival(zs, a).wait()
            keep[z, a] += zrecv[zs, a].astype(F32)

        if a is other:
            fsend[...] = keep[z, other].astype(BF)
            f_copy().start()

    out[:, pl.ds(pl.multiple_of(x * half, LANES), half)] = keep[z, x]
    f_copy().wait_recv()
    out[:, pl.ds(pl.multiple_of(other * half, LANES), half)] = frecv[...].astype(F32)

    f_copy().wait_send()
    lx_copy.wait_send()
    d_pass(core).wait_send()
    u_twin(core).wait_send()
    u_side.wait_send()
    for k in range(1, n):
        st_copy((me + k) % n, me).wait_send()
        lz_copy((me + k) % n, me).wait_send()

    @pl.loop(0, 9)
    def _(t):
        d_side(t).wait_send()

    @pl.when(hub)
    def _():
        for t in range(3):
            w_twin(t).wait_send()
            w_part(t, part).wait_send()
            w_pass(t, 0).wait_send()
            w_pass(t, 1).wait_send()

    @pl.when(jnp.logical_not(hub))
    def _():
        for t in range(3):
            w_side(t).wait_send()

    @pl.loop(0, zs)
    def _(s):
        x_fwd(s).wait_send()

        @pl.when(jnp.logical_and(s <= z, z < top))
        def _():
            u_col(0, s).wait_send()

        @pl.when(jnp.logical_and(s >= z, z > 0))
        def _():
            u_col(1, s).wait_send()

        for h in range(3):
            @pl.when(jnp.logical_and(s <= z, z < top))
            def _(h=h):
                a_copy(0, s, h).wait_send()

            @pl.when(jnp.logical_and(s >= z, z > 0))
            def _(h=h):
                a_copy(1, s, h).wait_send()

        @pl.when(s != z)
        def _():
            for a in range(2):
                z_copy(s, a).wait_send()


def run_block(n, steps, asked, row_of, hid, table, gain, bias, weight, down, up):
    cells, chans = hid.shape
    reqs = asked.shape[0]
    width = cells // reqs
    own = weight.shape[1]
    per, rank, _ = down.shape
    zs = n // 2
    half = chans // 2
    win = -(-2 * own // LANES) * LANES
    dma = pltpu.SemaphoreType.DMA
    vmem = pl.BlockSpec(memory_space=pltpu.VMEM)
    hbm = pl.BlockSpec(memory_space=pl.ANY)
    smem = pl.BlockSpec(memory_space=pltpu.SMEM)
    low = (cells // 2, 2 * rank)
    return pl.pallas_call(
        functools.partial(block_kernel, n, own, reqs, width, chans),
        out_shape=jax.ShapeDtypeStruct((cells, chans), F32),
        in_specs=[smem] * 3 + [vmem] * 4 + [hbm] * 3,
        out_specs=vmem,
        scratch_shapes=[
            pltpu.VMEM((zs, cells, chans), BF),
            pltpu.VMEM((zs, cells, win), BF),
            pltpu.VMEM((n + 2, cells, 3 * win), BF),
            pltpu.VMEM((3, 3, win, half), BF),
            pltpu.VMEM((2 * per, 3, 3 * rank, chans), BF),
            pltpu.VMEM((n * per, rank, half), BF),
            pltpu.VMEM((2, 8, LANES), F32),
            pltpu.VMEM((n, 2, 8, LANES), F32),
            pltpu.VMEM((zs, 2, cells, half), F32),
            pltpu.VMEM((zs, 2, cells, half), BF),
            pltpu.VMEM((zs + 1, 2, cells, half), BF),
            pltpu.VMEM((cells, half), BF),
            pltpu.VMEM((cells, half), BF),
            pltpu.VMEM((zs,) + low, F32),
            pltpu.VMEM((zs,) + low, BF),
            pltpu.VMEM((zs,) + low, BF),
            pltpu.VMEM((zs,) + low, BF),
            pltpu.VMEM((n,) + low, BF),
            pltpu.VMEM((2,) + low, BF),
            dma((n,)), dma((n,)),
            dma((3, 3)), dma((3, 3)), dma((3,)), dma((3,)), dma((3,)), dma((3,)), dma((3,)),
            dma((9,)), dma((9,)), dma((per, 9)), dma, dma,
            dma, dma, dma, dma((2, zs)), dma((zs,)), dma, dma,
            dma((2, zs, 3)), dma((zs, 3)), dma((zs,)), dma((zs,)),
            dma((zs, 2)), dma((zs + 1, 2)),
            dma, dma, dma((n,)), dma((n,)), dma, dma,
        ],
        compiler_params=pltpu.CompilerParams(
            collective_id=0, has_side_effects=True, vmem_limit_bytes=56 * 2**20
        ),
        cost_estimate=pl.CostEstimate(
            flops=2 * n * cells * 9 * win * half, bytes_accessed=10**8, transcendentals=0
        ),
    )(steps, asked, row_of, hid, table, gain, bias, weight.reshape((3, 3) + weight.shape[1:]), down, up)


def split_contraction(
    hidden, skip, timestep_embedding_table, timesteps, group_norm_gain, group_norm_bias,
    kernel_weight, adapter_down_weight, adapter_up_weight, request_adapter, adapter_row_table,
):
    shape = hidden.shape
    flat = (shape[0] * shape[1] * shape[2], shape[3])
    total = run_block(
        lax.axis_size("patch"), timesteps, request_adapter, adapter_row_table,
        hidden.reshape(flat), timestep_embedding_table, group_norm_gain, group_norm_bias,
        kernel_weight, adapter_down_weight, adapter_up_weight,
    )
    return skip + total.reshape(shape)


def fits(n, hidden, kernel_weight, down):
    own = kernel_weight.shape[1]
    return (
        n == 8 and hidden.shape[1] == 1 and hidden.shape[0] in (2, 4, 6, 8)
        and hidden.shape[3] == 1280 and own == 160 and down.shape[:2] == (2, 64)
    )


def broadcast(block, axis, owner):
    block = jnp.where(lax.axis_index(axis) == owner, block, jnp.zeros_like(block))
    return lax.psum(block, axis)


def padded(cells, sides, width):
    for axis, dim in sides:
        count = lax.axis_size(axis)
        ends = count - 1
        head = lax.slice_in_dim(cells, 0, width, axis=dim)
        tail = lax.slice_in_dim(cells, cells.shape[dim] - width, cells.shape[dim], axis=dim)
        cells = jnp.concatenate(
            [
                lax.ppermute(tail, axis, [(i, (i + 1) % count) for i in range(ends)]),
                cells,
                lax.ppermute(head, axis, [((i + 1) % count, i) for i in range(ends)]),
            ],
            axis=dim,
        )
    return cells


def from_partner(x, axis, stride):
    return lax.ppermute(x, axis, [(i, i ^ 1 << stride) for i in range(lax.axis_size(axis))])


def make_taps(extended, rows, width):
    pieces = [extended[:, dy : dy + rows, dx : dx + width, :] for dy in range(3) for dx in range(3)]
    stacked = jnp.stack(pieces, axis=3)
    count = stacked.shape[0] * rows * width
    return stacked.reshape(count, 9, stacked.shape[-1])


def load_adapter_factors(
    adapter_down_weight, adapter_up_weight, request_adapter, adapter_row_table, request_total
):
    resident_count = adapter_down_weight.shape[0]
    fetched = []
    for request in range(request_total):
        resident_row = adapter_row_table[request_adapter[request]]
        owner = resident_row // resident_count
        store_position = resident_row % resident_count
        resident_down = lax.dynamic_index_in_dim(
            adapter_down_weight, store_position, 0, keepdims=False
        )
        resident_up = lax.dynamic_index_in_dim(adapter_up_weight, store_position, 0, keepdims=False)
        fetched.append(
            (broadcast(resident_down, "patch", owner), broadcast(resident_up, "patch", owner))
        )
    return fetched


def shards(
    hidden,
    skip,
    timestep_embedding_table,
    timesteps,
    group_norm_gain,
    group_norm_bias,
    kernel_weight,
    adapter_down_weight,
    adapter_up_weight,
    request_adapter,
    adapter_row_table,
):
    request_total, rows, width, chans = hidden.shape
    steps_count = timestep_embedding_table.shape[0]
    onehot = (timesteps[:, None] == jnp.arange(steps_count, dtype=jnp.int32)[None, :]).astype(
        jnp.float32
    )
    temb = jnp.dot(
        onehot,
        timestep_embedding_table,
        preferred_element_type=jnp.float32,
        precision=lax.Precision.HIGHEST,
    )
    shifted = hidden + temb[:, None, None, :]
    grouped = shifted.reshape(request_total, rows, width, GROUPS, chans // GROUPS)
    count = rows * lax.axis_size("patch") * width * (chans // GROUPS)
    totals = lax.psum(jnp.sum(grouped, axis=(1, 2, 4)), "patch")
    mean = totals / count
    centered = grouped - mean[:, None, None, :, None]
    squares = lax.psum(jnp.sum(centered * centered, axis=(1, 2, 4)), "patch")
    var = squares / count
    normed = (centered * lax.rsqrt(var + 1e-05)[:, None, None, :, None]).reshape(
        request_total, rows, width, chans
    )
    act = jax.nn.silu(normed * group_norm_gain + group_norm_bias).astype(jnp.bfloat16)
    extended = padded(act, (("patch", 1),), 1)
    extended = jnp.pad(extended, ((0, 0), (0, 0), (1, 1), (0, 0)))
    partner = from_partner(extended, "req", 0)
    taps = make_taps(jnp.concatenate([extended, partner], axis=0), rows, width)
    pixels = request_total * rows * width
    conv_half = jnp.einsum(
        "ptc,tco->po",
        taps,
        lax.all_gather(kernel_weight, "patch", axis=1, tiled=True),
        preferred_element_type=jnp.float32,
    )
    own_half = conv_half[:pixels]
    returned = from_partner(conv_half[pixels:], "req", 0)
    first = lax.axis_index("req") == 0
    left_half = jnp.where(first, own_half, returned)
    right_half = jnp.where(first, returned, own_half)
    conv = jnp.concatenate([left_half, right_half], axis=1).reshape(
        request_total, rows * width, chans
    )
    own_taps = taps[:pixels].reshape(request_total, rows * width, 9 * chans)
    adapter_factors = load_adapter_factors(
        adapter_down_weight, adapter_up_weight, request_adapter, adapter_row_table, request_total
    )
    deltas = []
    for request in range(request_total):
        down_factor, upper_limit = adapter_factors[request]
        low = lax.dot_general(
            own_taps[request],
            down_factor,
            (((1,), (1,)), ((), ())),
            preferred_element_type=jnp.float32,
        ).astype(jnp.bfloat16)
        deltas.append(jnp.dot(low, upper_limit, preferred_element_type=jnp.float32))
    total = conv + jnp.stack(deltas, axis=0)
    return skip + total.reshape(request_total, rows, width, chans)


def solution(mesh):
    def step(*args):
        n = lax.axis_size("patch")
        if fits(n, args[0], args[6], args[7]):
            return split_contraction(*args)
        return shards(*args)

    return jax.shard_map(
        step,
        mesh=mesh,
        in_specs=(
            P(("groups", "req"), "patch", None, None),
            P(("groups", "req"), "patch", None, None),
            P(),
            P(("groups", "req")),
            P(),
            P(),
            P(None, "patch", "req"),
            P(("groups", "patch"), None, None),
            P(("groups", "patch"), None, None),
            P(("groups", "req")),
            P("groups"),
        ),
        out_specs=P(("groups", "req"), "patch", None, None),
        check_vma=False,
    )
```

```python
import functools

import jax
import jax.numpy as jnp
from jax import lax
from jax.experimental import pallas as pl
from jax.experimental.pallas import tpu as pltpu
from jax.sharding import PartitionSpec as P

GROUPS = 32
LANES = 128
WIN = 256
MESH = pl.DeviceIdType.MESH
BF = jnp.bfloat16
F32 = jnp.float32


def sum_dot(a, member, dims):
    parts, rest = [], a
    for _ in range(3):
        parts.append(rest.astype(BF))
        rest = rest - parts[-1].astype(F32)
    out = lax.dot_general(
        jnp.concatenate([p.astype(F32) for p in parts], axis=0).astype(BF), member, (dims, ((), ())),
        preferred_element_type=F32,
    )
    count = a.shape[0]
    return out[:count] + out[count : 2 * count] + out[2 * count :]


def block_kernel(
    n, own, reqs, width, chans,
    steps, asked, row_of, hid, table, gain, bias, w_hbm, d_hbm, u_hbm,
    out,
    rows, xin, taps, wpad, dall, uall, stat_out, stat_in, keep, zsend, zrecv,
    fsend, frecv, mine, lxs, lxr, lzs, lzr, lows,
    st_s, st_r, wc_s, wc_r, wx_s, wx_r, wy_s, wy_r, w_l, d_s, d_r, d_l, dp_s, dp_r,
    ux_s, ux_r, u_l, uz_s, uz_r, up_s, up_r, a_s, a_r, xf_s, xf_r,
    z_s, z_r, lx_s, lx_r, lz_s, lz_r, f_s, f_r,
):
    me = lax.axis_index("patch")
    core = lax.axis_index("req")
    mate = 1 - core
    zs = n // 2
    z, x = me // 2, me % 2
    other = 1 - x
    near = me + 1 - 2 * x
    hub = core == x
    half = chans // 2
    cells = reqs * width
    per, rank, _ = d_hbm.shape
    hrank = rank // 2
    win = xin.shape[2]
    top = zs - 1
    temb = [table[pl.ds(steps[r], 1), :] for r in range(reqs)]
    sel = [row_of[asked[r]] for r in range(reqs)]

    barrier = pltpu.get_barrier_semaphore()
    for k in range(1, n):
        pl.semaphore_signal(barrier, inc=1, device_id={"patch": (me + k) % n}, device_id_type=MESH)
    part = lax.axis_index("groups")
    for to in ({"req": mate}, {"groups": 1 - part}):
        pl.semaphore_signal(barrier, inc=1, device_id=to, device_id_type=MESH)
    pl.semaphore_wait(barrier, n + 1)

    def remote(src, dst, send, recv, to):
        return pltpu.make_async_remote_copy(
            src_ref=src, dst_ref=dst, send_sem=send, recv_sem=recv, device_id=to, device_id_type=MESH
        )

    side, twin, peer_part = {"patch": near}, {"req": mate}, {"groups": 1 - part}

    inner = pl.multiple_of((z % 2) * (win - 2 * own), 32)

    cut = own // 2

    def w_src(t, lo, size):
        return w_hbm.at[t, :, pl.ds(lo, size), :]

    def w_dst(t, j, lo, size):
        return wpad.at[t, :, pl.ds(pl.multiple_of(inner + j * own + lo, 16), size), :]

    def w_local(t):
        return pltpu.make_async_copy(w_src(t, 0, own), w_dst(t, x, 0, own), w_l.at[t])

    def w_twin(t):
        return remote(w_src(t, 0, own), w_dst(t, x, 0, own), wc_s.at[0, t], wc_r.at[0, t], twin)

    def w_side(t):
        lo = pl.multiple_of(part * cut, 16)
        return remote(w_src(t, lo, cut), w_dst(t, x, lo, cut), wx_s.at[t], wx_r.at[t], side)

    def w_part(t, from_part):
        block = w_dst(t, other, pl.multiple_of(from_part * cut, 16), cut)
        return remote(block, block, wy_s.at[t], wy_r.at[t], peer_part)

    def w_pass(t, from_part):
        block = w_dst(t, other, pl.multiple_of(from_part * cut, 16), cut)
        return remote(block, block, wc_s.at[1 + from_part, t], wc_r.at[1 + from_part, t], twin)

    rank_at = pl.multiple_of(core * hrank, hrank)

    def u_src(c):
        return u_hbm.at[:, pl.ds(rank_at, hrank), pl.ds(pl.multiple_of(c * half, LANES), half)]

    def u_dst(at, count):
        return uall.at[pl.ds(at, count), pl.ds(rank_at, hrank), :]

    u_own = pltpu.make_async_copy(u_src(x), u_dst(me * per, per), u_l)
    u_side = remote(u_src(other), u_dst(me * per, per), ux_s, ux_r, side)

    def u_col(way, src):
        block = u_dst(src * 2 * per, 2 * per)
        return remote(block, block, uz_s.at[way, src], uz_r.at[src], {"patch": me + 2 - 4 * way})

    def u_hop(k):
        @pl.when(z >= k)
        def _():
            u_col(0, z - k).wait_recv()

            @pl.when(z < top)
            def _():
                u_col(0, z - k).start()

        @pl.when(z + k <= top)
        def _():
            u_col(1, z + k).wait_recv()

            @pl.when(z > 0)
            def _():
                u_col(1, z + k).start()

    lane = pl.multiple_of(z * 2 * own // LANES * LANES, LANES)

    def d_src(a, t, lo, size):
        tap = t % 3 * 3 + t // 3
        return d_hbm.at[a, :, pl.ds(pl.multiple_of(tap * chans + lo, LANES), size)]

    def d_dst(j, a, t, lo, size):
        at = pl.ds(pl.multiple_of((t % 3) * rank, rank), rank)
        return dall.at[j * per + a, t // 3, at, pl.ds(lo, size)]

    def d_own(a, t):
        return pltpu.make_async_copy(d_src(a, t, 0, chans), d_dst(x, a, t, 0, chans), d_l.at[a, t])

    def d_side(at, t):
        first = at * 2 * own // LANES * LANES
        sides = ((0, first), (first + win, chans - first - win))
        return [
            remote(
                d_src(core, t, lo, size), d_dst(x, core, t, lo, size), d_s.at[t, i], d_r.at[t, i], side
            )
            for i, (lo, size) in enumerate(sides)
            if size > 0
        ]

    def d_pass(a, dx):
        block = dall.at[other * per + a, dx]
        return remote(block, block, dp_s.at[dx], dp_r.at[dx], twin)

    u_own.start()
    u_side.start()

    @pl.when(hub)
    def _():
        for t in range(3):
            w_local(t).start()
            w_twin(t).start()

    @pl.when(jnp.logical_not(hub))
    def _():
        for t in range(3):
            w_side(t).start()

    for a in range(per):
        @pl.loop(0, 9)
        def _(t, a=a):
            d_own(a, t).start()

    spare = pl.multiple_of((1 - z % 2) * 2 * own, 32)
    wpad[:, :, pl.ds(spare, win - 2 * own), :] = jnp.zeros((3, 3, win - 2 * own, half), BF)

    dall[other * per + core, :, :, pl.ds(lane, win)] = jnp.zeros((3, 3 * rank, win), BF)
    c_of = lax.broadcasted_iota(jnp.int32, (chans, LANES), 0)
    g_of = lax.broadcasted_iota(jnp.int32, (chans, LANES), 1)
    size = chans // GROUPS
    member = jnp.where((c_of >= g_of * size) & (c_of < (g_of + 1) * size), 1.0, 0.0).astype(BF)
    count = width * size
    sums = [
        jnp.sum(hid[r * width : (r + 1) * width, :] + temb[r], axis=0, keepdims=True)
        for r in range(reqs)
    ]
    pad = [jnp.zeros((8 - reqs, chans), F32)] if reqs < 8 else []
    mean = sum_dot(jnp.concatenate(sums + pad, axis=0), member, ((1,), (0,))) / count
    wide = sum_dot(mean, member, ((1,), (1,)))
    squares = []
    for r in range(reqs):
        c = hid[r * width : (r + 1) * width, :] + temb[r] - wide[r : r + 1, :]
        squares.append(jnp.sum(c * c, axis=0, keepdims=True))
    second = sum_dot(jnp.concatenate(squares + pad, axis=0), member, ((1,), (0,)))
    stat_out[0] = mean
    stat_out[1] = second

    def st_copy(peer, src):
        return remote(stat_out, stat_in.at[src], st_s.at[peer], st_r.at[src], {"patch": peer})

    for k in range(1, n):
        st_copy((me + k) % n, me).start()
    stat_in[me] = stat_out[...]
    u_own.wait()
    u_side.wait_recv()

    @pl.when(z < top)
    def _():
        u_col(0, z).start()

    @pl.when(z > 0)
    def _():
        u_col(1, z).start()

    for k in range(1, n):
        st_copy((me + k) % n, (me + k) % n).wait_recv()
    means = stat_in[:, 0]
    total_mean = jnp.sum(means, axis=0) / n
    spread = means - total_mean[None]
    var = (jnp.sum(stat_in[:, 1], axis=0) + count * jnp.sum(spread * spread, axis=0)) / (count * n)
    mean_w = sum_dot(total_mean, member, ((1,), (1,)))
    inv_w = sum_dot(lax.rsqrt(var + 1e-05), member, ((1,), (1,)))
    scale = gain[...].reshape(1, chans)
    shift = bias[...].reshape(1, chans)
    for r in range(reqs):
        at = slice(r * width, (r + 1) * width)
        v = (hid[at, :] + temb[r] - mean_w[r : r + 1, :]) * inv_w[r : r + 1, :]
        v = v * scale + shift
        rows[z, at, :] = (v / (1.0 + jnp.exp(-v))).astype(BF)

    spans = (
        ((chans - win, win), (half, half - win), (0, half)),
        ((0, win), (win, half - win), (half, half)),
    )

    def a_copy(way, s, m):
        block = rows.at[s, :, pl.ds(*spans[way][m])]
        to = {"patch": me + 2 - 4 * way}
        return remote(block, block, a_s.at[way, s, m], a_r.at[s, m], to)

    def back(way, k):
        return z + k if way else z - k

    def hop(way, k, m):
        a_copy(way, back(way, k), m).wait_recv()

        @pl.when(middle)
        def _():
            a_copy(way, back(way, k), m).start()

    def x_fwd(s):
        return remote(rows.at[s, :, pl.ds(lane, win)], xin.at[s], xf_s.at[s], xf_r.at[s], side)

    px = lax.broadcasted_iota(jnp.int32, (cells, win), 0) % width

    def lay(y, v):
        v = v.astype(F32)
        taps[y + 1, :, 0:win] = jnp.where(px == 0, 0.0, pltpu.roll(v, 1, 0)).astype(BF)
        taps[y + 1, :, win : 2 * win] = v.astype(BF)
        taps[y + 1, :, 2 * win :] = jnp.where(px == width - 1, 0.0, pltpu.roll(v, cells - 1, 0)).astype(BF)

    def got(s):
        x_fwd(s).start()
        lay(2 * s + x, rows[s, :, pl.ds(lane, win)])

    def share_weights():
        @pl.when(hub)
        def _():
            for t in range(3):
                w_side(t).wait_recv()
                w_part(t, part).start()
                w_pass(t, part).start()

    def send_down(at, lo, hi):
        @pl.loop(lo, hi)
        def _(t):
            for copy in d_side(at, t):
                copy.start()

    end = jnp.logical_or(z == 0, z == top)
    middle = jnp.logical_not(end)

    @pl.when(z < top)
    def _():
        a_copy(0, z, 0).start()

    @pl.when(z > 0)
    def _():
        a_copy(1, z, 0).start()

    got(z)
    taps[0] = jnp.zeros(taps.shape[1:], BF)
    taps[n + 1] = jnp.zeros(taps.shape[1:], BF)

    def at_end(at, way):
        for m in (1, 2):
            a_copy(1 - way, z, m).start()
        for k in range(1, zs):
            hop(way, k, 0)
            got(back(way, k))
            if k == 1:
                share_weights()
        send_down(at, 0, 9)

    def at_middle(at, way):
        send_down(at, 0, 3)
        hop(1 - way, 1, 0)
        hop(way, 1, 0)
        a_copy(way, z, 1).start()
        share_weights()
        hop(1 - way, 2, 0)
        a_copy(1 - way, z, 1).start()
        hop(way, 1, 1)
        for k in (1, 2):
            hop(1 - way, k, 1)
            got(back(1 - way, k))
        for to in (way, 1 - way):
            a_copy(to, z, 2).start()
        hop(way, 1, 2)
        got(back(way, 1))
        send_down(at, 3, 9)

    for at, place, way in ((0, at_end, 1), (1, at_middle, 0), (2, at_middle, 1), (3, at_end, 0)):
        @pl.when(z == at)
        def _(place=place, at=at, way=way):
            place(at, way)

    @pl.when(hub)
    def _():
        for t in range(3):
            w_part(t, 1 - part).wait_recv()
            w_pass(t, 1 - part).start()

    @pl.loop(0, zs)
    def _(s):
        x_fwd(s).wait_recv()
        lay(2 * s + other, xin[s])

    @pl.when(hub)
    def _():
        for t in range(3):
            w_local(t).wait()

    @pl.when(jnp.logical_not(hub))
    def _():
        for t in range(3):
            w_twin(t).wait_recv()
            w_pass(t, 0).wait_recv()
            w_pass(t, 1).wait_recv()

    order = (3 * (1 - z // 2), (2 + 3 * z) % 5, 1 + z % 2, z)

    def conv(dest):
        for lo in range(0, half, WIN):
            hi = min(lo + WIN, half)
            s = jnp.zeros((2 * cells, hi - lo), F32)
            for dy in range(3):
                lhs = taps[pl.ds(2 * dest + dy, 2)].reshape(2 * cells, 3 * win)
                rhs = wpad[dy, :, :, lo:hi].reshape(3 * win, hi - lo)
                s += jnp.dot(lhs, rhs, preferred_element_type=F32)
            keep[dest, :, :, lo:hi] = s.reshape(2, cells, hi - lo)

    def z_copy(dest, a):
        after = jnp.where(dest > z, z + 1, z - 1)
        at = jnp.where(jnp.logical_and(dest < z, after == dest), zs, dest)
        return remote(
            zsend.at[dest, a], zrecv.at[at, a], z_s.at[dest, a], z_r.at[at, a], {"patch": after * 2 + x}
        )

    def z_arrival(at, a):
        return pltpu.make_async_copy(zrecv.at[at, a], zrecv.at[at, a], z_r.at[at, a])

    def push(dest, a):
        upward = jnp.logical_and(dest > z, z > 0)
        downward = jnp.logical_and(dest < z, z < top)

        @pl.when(jnp.logical_or(upward, downward))
        def _():
            z_arrival(dest, a).wait()
            keep[dest, a] += zrecv[dest, a].astype(F32)

        zsend[dest, a] = keep[dest, a].astype(BF)
        z_copy(dest, a).start()

    def conv_row(dest, a):
        for lo in range(0, half, WIN):
            hi = min(lo + WIN, half)
            s = jnp.zeros((cells, hi - lo), F32)
            for dy in range(3):
                rhs = wpad[dy, :, :, lo:hi].reshape(3 * win, hi - lo)
                s += jnp.dot(taps[2 * dest + a + dy], rhs, preferred_element_type=F32)
            keep[dest, a, :, lo:hi] = s

    for i in range(zs):
        if i == 0:
            conv_row(order[0], other)

            @pl.when(end)
            def _():
                push(order[0], other)

            conv_row(order[0], x)
        else:
            conv(order[i])
        if i < 2:
            for at, way in ((1, 1), (2, 0)):
                @pl.when(z == at)
                def _(i=i, way=way):
                    hop(way, i + 1, 2)

            @pl.when(middle)
            def _(i=i):
                u_hop(i + 1)
        if i == 0:
            @pl.when(middle)
            def _():
                push(order[0], other)
        elif i < zs - 1:
            push(order[i], other)
        if i < zs - 1:
            if i < zs - 2:
                push(order[i], x)

    @pl.when(end)
    def _():
        u_hop(1)
        u_hop(2)

    for at, way in ((0, 1), (top, 0)):
        @pl.when(z == at)
        def _(way=way):
            for k in range(1, zs):
                for m in (1, 2):
                    a_copy(way, back(way, k), m).wait_recv()

    for dx in range(3):
        for at in range(zs):
            @pl.when(z == at)
            def _(at=at, dx=dx):
                @pl.loop(3 * dx, 3 * dx + 3)
                def _(t):
                    for copy in d_side(at, t):
                        copy.wait_recv()

        d_pass(core, dx).start()
    for a in range(per):
        @pl.loop(0, 9)
        def _(t, a=a):
            d_own(a, t).wait()

    u_hop(3)

    def u_twin(at):
        part = uall.at[:, pl.ds(pl.multiple_of(at * hrank, hrank), hrank), :]
        return remote(part, part, up_s, up_r, twin)

    u_twin(core).start()
    for dx in range(3):
        d_pass(mate, dx).wait_recv()

    pq = lax.broadcasted_iota(jnp.int32, (zs * width, 3 * rank), 0) % width
    none = jnp.zeros((1, width, rank), F32)

    def products(lhs, rhs):
        prod = [
            lax.dot_general(lhs, rhs(dx), (((1,), (1,)), ((), ())), preferred_element_type=F32)
            for dx in range(3)
        ]
        s = prod[1]
        s += jnp.where(pq == 0, 0.0, pltpu.roll(prod[0], 1, 0))
        s += jnp.where(pq == width - 1, 0.0, pltpu.roll(prod[2], zs * width - 1, 0))
        s = s.reshape(zs, width, 3 * rank)
        above, level, below = s[:, :, :rank], s[:, :, rank : 2 * rank], s[:, :, 2 * rank :]
        even = above + jnp.concatenate([below[1:], none], axis=0)
        odd = jnp.concatenate([none, above[:-1]], axis=0) + below
        return level, even, odd

    for q in range(reqs // 2):
        pair_mine, pair_side = [], []
        for r in (2 * q, 2 * q + 1):
            stored = sel[r] - z * 2 * per
            here = jnp.logical_and(stored >= 0, stored < 2 * per)
            index = jnp.clip(stored, 0, 2 * per - 1)
            at = slice(r * width, (r + 1) * width)
            level, even, odd = products(
                rows[:, at, :].reshape(zs * width, chans), lambda dx: dall[index, dx]
            )
            level2, even2, odd2 = products(
                xin[:, at, :].reshape(zs * width, win), lambda dx: dall[index, dx, :, pl.ds(lane, win)]
            )
            first = x == 0
            pair_mine.append(jnp.where(here, level + jnp.where(first, odd2, even2), 0.0))
            pair_side.append(jnp.where(here, level2 + jnp.where(first, even, odd), 0.0))
        at = slice(q * width, (q + 1) * width)
        mine[:, at, :] = jnp.concatenate(pair_mine, axis=2)
        lxs[:, at, :] = jnp.concatenate(pair_side, axis=2).astype(BF)

    lx_copy = remote(lxs, lxr, lx_s, lx_r, side)
    lx_copy.start()

    def lz_copy(peer, src):
        return remote(lzs.at[peer // 2], lzr.at[src], lz_s.at[peer], lz_r.at[src], {"patch": peer})

    lx_copy.wait_recv()
    lzs[...] = (mine[...] + lxr[...].astype(F32)).astype(BF)
    for k in range(1, n):
        lz_copy((me + k) % n, me).start()

    push(order[zs - 2], x)
    lzr[me] = lzs[z]
    for k in range(1, n):
        lz_copy((me + k) % n, (me + k) % n).wait_recv()
    for a in range(2):
        low = lzr[a].astype(F32)
        for k in range(1, zs):
            low += lzr[2 * k + a].astype(F32)
        lows[a] = low.astype(BF)
    u_twin(mate).wait_recv()

    def f_copy():
        return remote(fsend, frecv, f_s, f_r, side)

    for a in (other, x):
        for r in range(reqs):
            low = lows[a, r // 2 * width : (r // 2 + 1) * width, r % 2 * rank : (r % 2 + 1) * rank]
            at = slice(r * width, (r + 1) * width)
            keep[z, a, at, :] += jnp.dot(low, uall[sel[r]], preferred_element_type=F32)

        @pl.when(z > 0)
        def _(a=a):
            z_arrival(z, a).wait()
            keep[z, a] += zrecv[z, a].astype(F32)

        @pl.when(z < top)
        def _(a=a):
            z_arrival(zs, a).wait()
            keep[z, a] += zrecv[zs, a].astype(F32)

        if a is other:
            fsend[...] = keep[z, other].astype(BF)
            f_copy().start()

    out[:, pl.ds(pl.multiple_of(x * half, LANES), half)] = keep[z, x]
    f_copy().wait_recv()
    out[:, pl.ds(pl.multiple_of(other * half, LANES), half)] = frecv[...].astype(F32)

    f_copy().wait_send()
    lx_copy.wait_send()
    for dx in range(3):
        d_pass(core, dx).wait_send()
    u_twin(core).wait_send()
    u_side.wait_send()
    for k in range(1, n):
        st_copy((me + k) % n, me).wait_send()
        lz_copy((me + k) % n, me).wait_send()

    for at in range(zs):
        @pl.when(z == at)
        def _(at=at):
            @pl.loop(0, 9)
            def _(t):
                for copy in d_side(at, t):
                    copy.wait_send()

    @pl.when(hub)
    def _():
        for t in range(3):
            w_twin(t).wait_send()
            w_part(t, part).wait_send()
            w_pass(t, 0).wait_send()
            w_pass(t, 1).wait_send()

    @pl.when(jnp.logical_not(hub))
    def _():
        for t in range(3):
            w_side(t).wait_send()

    @pl.loop(0, zs)
    def _(s):
        x_fwd(s).wait_send()

        @pl.when(jnp.logical_and(s <= z, z < top))
        def _():
            u_col(0, s).wait_send()

        @pl.when(jnp.logical_and(s >= z, z > 0))
        def _():
            u_col(1, s).wait_send()

        for h in range(3):
            @pl.when(jnp.logical_and(s <= z, z < top))
            def _(h=h):
                a_copy(0, s, h).wait_send()

            @pl.when(jnp.logical_and(s >= z, z > 0))
            def _(h=h):
                a_copy(1, s, h).wait_send()

        @pl.when(s != z)
        def _():
            for a in range(2):
                z_copy(s, a).wait_send()


def run_block(n, steps, asked, row_of, hid, table, gain, bias, weight, down, up):
    cells, chans = hid.shape
    reqs = asked.shape[0]
    width = cells // reqs
    own = weight.shape[1]
    per, rank, _ = down.shape
    zs = n // 2
    half = chans // 2
    win = -(-2 * own // LANES) * LANES
    dma = pltpu.SemaphoreType.DMA
    vmem = pl.BlockSpec(memory_space=pltpu.VMEM)
    hbm = pl.BlockSpec(memory_space=pl.ANY)
    smem = pl.BlockSpec(memory_space=pltpu.SMEM)
    low = (cells // 2, 2 * rank)
    return pl.pallas_call(
        functools.partial(block_kernel, n, own, reqs, width, chans),
        out_shape=jax.ShapeDtypeStruct((cells, chans), F32),
        in_specs=[smem] * 3 + [vmem] * 4 + [hbm] * 3,
        out_specs=vmem,
        scratch_shapes=[
            pltpu.VMEM((zs, cells, chans), BF),
            pltpu.VMEM((zs, cells, win), BF),
            pltpu.VMEM((n + 2, cells, 3 * win), BF),
            pltpu.VMEM((3, 3, win, half), BF),
            pltpu.VMEM((2 * per, 3, 3 * rank, chans), BF),
            pltpu.VMEM((n * per, rank, half), BF),
            pltpu.VMEM((2, 8, LANES), F32),
            pltpu.VMEM((n, 2, 8, LANES), F32),
            pltpu.VMEM((zs, 2, cells, half), F32),
            pltpu.VMEM((zs, 2, cells, half), BF),
            pltpu.VMEM((zs + 1, 2, cells, half), BF),
            pltpu.VMEM((cells, half), BF),
            pltpu.VMEM((cells, half), BF),
            pltpu.VMEM((zs,) + low, F32),
            pltpu.VMEM((zs,) + low, BF),
            pltpu.VMEM((zs,) + low, BF),
            pltpu.VMEM((zs,) + low, BF),
            pltpu.VMEM((n,) + low, BF),
            pltpu.VMEM((2,) + low, BF),
            dma((n,)), dma((n,)),
            dma((3, 3)), dma((3, 3)), dma((3,)), dma((3,)), dma((3,)), dma((3,)), dma((3,)),
            dma((9, 2)), dma((9, 2)), dma((per, 9)), dma((3,)), dma((3,)),
            dma, dma, dma, dma((2, zs)), dma((zs,)), dma, dma,
            dma((2, zs, 3)), dma((zs, 3)), dma((zs,)), dma((zs,)),
            dma((zs, 2)), dma((zs + 1, 2)),
            dma, dma, dma((n,)), dma((n,)), dma, dma,
        ],
        compiler_params=pltpu.CompilerParams(
            collective_id=0, has_side_effects=True, vmem_limit_bytes=56 * 2**20
        ),
        cost_estimate=pl.CostEstimate(
            flops=2 * n * cells * 9 * win * half, bytes_accessed=10**8, transcendentals=0
        ),
    )(steps, asked, row_of, hid, table, gain, bias, weight.reshape((3, 3) + weight.shape[1:]), down, up)


def split_contraction(
    hidden, skip, timestep_embedding_table, timesteps, group_norm_gain, group_norm_bias,
    kernel_weight, adapter_down_weight, adapter_up_weight, request_adapter, adapter_row_table,
):
    shape = hidden.shape
    flat = (shape[0] * shape[1] * shape[2], shape[3])
    total = run_block(
        lax.axis_size("patch"), timesteps, request_adapter, adapter_row_table,
        hidden.reshape(flat), timestep_embedding_table, group_norm_gain, group_norm_bias,
        kernel_weight, adapter_down_weight, adapter_up_weight,
    )
    return skip + total.reshape(shape)


def fits(n, hidden, kernel_weight, down):
    own = kernel_weight.shape[1]
    return (
        n == 8 and hidden.shape[1] == 1 and hidden.shape[0] in (2, 4, 6, 8)
        and hidden.shape[3] == 1280 and own == 160 and down.shape[:2] == (2, 64)
    )


def broadcast(block, axis, owner):
    block = jnp.where(lax.axis_index(axis) == owner, block, jnp.zeros_like(block))
    return lax.psum(block, axis)


def padded(cells, sides, width):
    for axis, dim in sides:
        count = lax.axis_size(axis)
        ends = count - 1
        head = lax.slice_in_dim(cells, 0, width, axis=dim)
        tail = lax.slice_in_dim(cells, cells.shape[dim] - width, cells.shape[dim], axis=dim)
        cells = jnp.concatenate(
            [
                lax.ppermute(tail, axis, [(i, (i + 1) % count) for i in range(ends)]),
                cells,
                lax.ppermute(head, axis, [((i + 1) % count, i) for i in range(ends)]),
            ],
            axis=dim,
        )
    return cells


def from_partner(x, axis, stride):
    return lax.ppermute(x, axis, [(i, i ^ 1 << stride) for i in range(lax.axis_size(axis))])


def make_taps(extended, rows, width):
    pieces = [extended[:, dy : dy + rows, dx : dx + width, :] for dy in range(3) for dx in range(3)]
    stacked = jnp.stack(pieces, axis=3)
    count = stacked.shape[0] * rows * width
    return stacked.reshape(count, 9, stacked.shape[-1])


def load_adapter_factors(
    adapter_down_weight, adapter_up_weight, request_adapter, adapter_row_table, request_total
):
    resident_count = adapter_down_weight.shape[0]
    fetched = []
    for request in range(request_total):
        resident_row = adapter_row_table[request_adapter[request]]
        owner = resident_row // resident_count
        store_position = resident_row % resident_count
        resident_down = lax.dynamic_index_in_dim(
            adapter_down_weight, store_position, 0, keepdims=False
        )
        resident_up = lax.dynamic_index_in_dim(adapter_up_weight, store_position, 0, keepdims=False)
        fetched.append(
            (broadcast(resident_down, "patch", owner), broadcast(resident_up, "patch", owner))
        )
    return fetched


def shards(
    hidden,
    skip,
    timestep_embedding_table,
    timesteps,
    group_norm_gain,
    group_norm_bias,
    kernel_weight,
    adapter_down_weight,
    adapter_up_weight,
    request_adapter,
    adapter_row_table,
):
    request_total, rows, width, chans = hidden.shape
    steps_count = timestep_embedding_table.shape[0]
    onehot = (timesteps[:, None] == jnp.arange(steps_count, dtype=jnp.int32)[None, :]).astype(
        jnp.float32
    )
    temb = jnp.dot(
        onehot,
        timestep_embedding_table,
        preferred_element_type=jnp.float32,
        precision=lax.Precision.HIGHEST,
    )
    shifted = hidden + temb[:, None, None, :]
    grouped = shifted.reshape(request_total, rows, width, GROUPS, chans // GROUPS)
    count = rows * lax.axis_size("patch") * width * (chans // GROUPS)
    totals = lax.psum(jnp.sum(grouped, axis=(1, 2, 4)), "patch")
    mean = totals / count
    centered = grouped - mean[:, None, None, :, None]
    squares = lax.psum(jnp.sum(centered * centered, axis=(1, 2, 4)), "patch")
    var = squares / count
    normed = (centered * lax.rsqrt(var + 1e-05)[:, None, None, :, None]).reshape(
        request_total, rows, width, chans
    )
    act = jax.nn.silu(normed * group_norm_gain + group_norm_bias).astype(jnp.bfloat16)
    extended = padded(act, (("patch", 1),), 1)
    extended = jnp.pad(extended, ((0, 0), (0, 0), (1, 1), (0, 0)))
    partner = from_partner(extended, "req", 0)
    taps = make_taps(jnp.concatenate([extended, partner], axis=0), rows, width)
    pixels = request_total * rows * width
    conv_half = jnp.einsum(
        "ptc,tco->po",
        taps,
        lax.all_gather(kernel_weight, "patch", axis=1, tiled=True),
        preferred_element_type=jnp.float32,
    )
    own_half = conv_half[:pixels]
    returned = from_partner(conv_half[pixels:], "req", 0)
    first = lax.axis_index("req") == 0
    left_half = jnp.where(first, own_half, returned)
    right_half = jnp.where(first, returned, own_half)
    conv = jnp.concatenate([left_half, right_half], axis=1).reshape(
        request_total, rows * width, chans
    )
    own_taps = taps[:pixels].reshape(request_total, rows * width, 9 * chans)
    adapter_factors = load_adapter_factors(
        adapter_down_weight, adapter_up_weight, request_adapter, adapter_row_table, request_total
    )
    deltas = []
    for request in range(request_total):
        down_factor, upper_limit = adapter_factors[request]
        low = lax.dot_general(
            own_taps[request],
            down_factor,
            (((1,), (1,)), ((), ())),
            preferred_element_type=jnp.float32,
        ).astype(jnp.bfloat16)
        deltas.append(jnp.dot(low, upper_limit, preferred_element_type=jnp.float32))
    total = conv + jnp.stack(deltas, axis=0)
    return skip + total.reshape(request_total, rows, width, chans)


def solution(mesh):
    def step(*args):
        n = lax.axis_size("patch")
        if fits(n, args[0], args[6], args[7]):
            return split_contraction(*args)
        return shards(*args)

    return jax.shard_map(
        step,
        mesh=mesh,
        in_specs=(
            P(("groups", "req"), "patch", None, None),
            P(("groups", "req"), "patch", None, None),
            P(),
            P(("groups", "req")),
            P(),
            P(),
            P(None, "patch", "req"),
            P(("groups", "patch"), None, None),
            P(("groups", "patch"), None, None),
            P(("groups", "req")),
            P("groups"),
        ),
        out_specs=P(("groups", "req"), "patch", None, None),
        check_vma=False,
    )
```

```python
import functools

import jax
import jax.numpy as jnp
from jax import lax
from jax.experimental import pallas as pl
from jax.experimental.pallas import tpu as pltpu
from jax.sharding import PartitionSpec as P

GROUPS = 32
LANES = 128
WIN = 256
MESH = pl.DeviceIdType.MESH
BF = jnp.bfloat16
F32 = jnp.float32


def sum_dot(a, member, dims):
    parts, rest = [], a
    for _ in range(3):
        parts.append(rest.astype(BF))
        rest = rest - parts[-1].astype(F32)
    out = lax.dot_general(
        jnp.concatenate([p.astype(F32) for p in parts], axis=0).astype(BF), member, (dims, ((), ())),
        preferred_element_type=F32,
    )
    count = a.shape[0]
    return out[:count] + out[count : 2 * count] + out[2 * count :]


def block_kernel(
    n, own, reqs, width, chans,
    steps, asked, row_of, hid, table, gain, bias, w_hbm, d_hbm, u_hbm,
    out,
    rows, xin, taps, wpad, dall, uall, stat_out, stat_in, keep, zsend, zrecv,
    fsend, frecv, mine, lxs, lxr, lzs, lzr, lows,
    st_s, st_r, wc_s, wc_r, wx_s, wx_r, wy_s, wy_r, w_l, d_s, d_r, d_l, dp_s, dp_r,
    ux_s, ux_r, u_l, uz_s, uz_r, up_s, up_r, a_s, a_r, xf_s, xf_r,
    z_s, z_r, lx_s, lx_r, lz_s, lz_r, f_s, f_r,
):
    me = lax.axis_index("patch")
    core = lax.axis_index("req")
    mate = 1 - core
    zs = n // 2
    z, x = me // 2, me % 2
    other = 1 - x
    near = me + 1 - 2 * x
    hub = core == x
    half = chans // 2
    cells = reqs * width
    per, rank, _ = d_hbm.shape
    hrank = rank // 2
    win = xin.shape[2]
    top = zs - 1
    temb = [table[pl.ds(steps[r], 1), :] for r in range(reqs)]
    sel = [row_of[asked[r]] for r in range(reqs)]

    barrier = pltpu.get_barrier_semaphore()
    for k in range(1, n):
        pl.semaphore_signal(barrier, inc=1, device_id={"patch": (me + k) % n}, device_id_type=MESH)
    part = lax.axis_index("groups")
    for to in ({"req": mate}, {"groups": 1 - part}):
        pl.semaphore_signal(barrier, inc=1, device_id=to, device_id_type=MESH)
    pl.semaphore_wait(barrier, n + 1)

    def remote(src, dst, send, recv, to):
        return pltpu.make_async_remote_copy(
            src_ref=src, dst_ref=dst, send_sem=send, recv_sem=recv, device_id=to, device_id_type=MESH
        )

    side, twin, peer_part = {"patch": near}, {"req": mate}, {"groups": 1 - part}

    inner = pl.multiple_of((z % 2) * (win - 2 * own), 32)

    cut = own // 2

    def w_src(t, lo, size):
        return w_hbm.at[t, :, pl.ds(lo, size), :]

    def w_dst(t, j, lo, size):
        return wpad.at[t, :, pl.ds(pl.multiple_of(inner + j * own + lo, 16), size), :]

    def w_local(t):
        return pltpu.make_async_copy(w_src(t, 0, own), w_dst(t, x, 0, own), w_l.at[t])

    def w_twin(t):
        return remote(w_src(t, 0, own), w_dst(t, x, 0, own), wc_s.at[0, t], wc_r.at[0, t], twin)

    def w_side(t):
        lo = pl.multiple_of(part * cut, 16)
        return remote(w_src(t, lo, cut), w_dst(t, x, lo, cut), wx_s.at[t], wx_r.at[t], side)

    def w_part(t, from_part):
        block = w_dst(t, other, pl.multiple_of(from_part * cut, 16), cut)
        return remote(block, block, wy_s.at[t], wy_r.at[t], peer_part)

    def w_pass(t, from_part):
        block = w_dst(t, other, pl.multiple_of(from_part * cut, 16), cut)
        return remote(block, block, wc_s.at[1 + from_part, t], wc_r.at[1 + from_part, t], twin)

    rank_at = pl.multiple_of(core * hrank, hrank)

    def u_src(c):
        return u_hbm.at[:, pl.ds(rank_at, hrank), pl.ds(pl.multiple_of(c * half, LANES), half)]

    def u_dst(at, count):
        return uall.at[pl.ds(at, count), pl.ds(rank_at, hrank), :]

    u_own = pltpu.make_async_copy(u_src(x), u_dst(me * per, per), u_l)
    u_side = remote(u_src(other), u_dst(me * per, per), ux_s, ux_r, side)

    def u_col(way, src):
        block = u_dst(src * 2 * per, 2 * per)
        return remote(block, block, uz_s.at[way, src], uz_r.at[src], {"patch": me + 2 - 4 * way})

    def u_hop(k):
        @pl.when(z >= k)
        def _():
            u_col(0, z - k).wait_recv()

            @pl.when(z < top)
            def _():
                u_col(0, z - k).start()

        @pl.when(z + k <= top)
        def _():
            u_col(1, z + k).wait_recv()

            @pl.when(z > 0)
            def _():
                u_col(1, z + k).start()

    lane = pl.multiple_of(z * 2 * own // LANES * LANES, LANES)

    def d_src(a, t, lo, size):
        tap = t % 3 * 3 + t // 3
        return d_hbm.at[a, :, pl.ds(pl.multiple_of(tap * chans + lo, LANES), size)]

    def d_dst(j, a, t, lo, size):
        at = pl.ds(pl.multiple_of((t % 3) * rank, rank), rank)
        return dall.at[j * per + a, t // 3, at, pl.ds(lo, size)]

    def d_own(a, t):
        return pltpu.make_async_copy(d_src(a, t, 0, chans), d_dst(x, a, t, 0, chans), d_l.at[a, t])

    def d_side(at, t):
        first = at * 2 * own // LANES * LANES
        sides = ((0, first), (first + win, chans - first - win))
        return [
            remote(
                d_src(core, t, lo, size), d_dst(x, core, t, lo, size), d_s.at[t, i], d_r.at[t, i], side
            )
            for i, (lo, size) in enumerate(sides)
            if size > 0
        ]

    def d_pass(a, dx):
        block = dall.at[other * per + a, dx]
        return remote(block, block, dp_s.at[dx], dp_r.at[dx], twin)

    u_own.start()
    u_side.start()

    @pl.when(hub)
    def _():
        for t in range(3):
            w_local(t).start()
            w_twin(t).start()

    @pl.when(jnp.logical_not(hub))
    def _():
        for t in range(3):
            w_side(t).start()

    for a in range(per):
        @pl.loop(0, 9)
        def _(t, a=a):
            d_own(a, t).start()

    spare = pl.multiple_of((1 - z % 2) * 2 * own, 32)
    wpad[:, :, pl.ds(spare, win - 2 * own), :] = jnp.zeros((3, 3, win - 2 * own, half), BF)

    dall[other * per + core, :, :, pl.ds(lane, win)] = jnp.zeros((3, 3 * rank, win), BF)
    c_of = lax.broadcasted_iota(jnp.int32, (chans, LANES), 0)
    g_of = lax.broadcasted_iota(jnp.int32, (chans, LANES), 1)
    size = chans // GROUPS
    member = jnp.where((c_of >= g_of * size) & (c_of < (g_of + 1) * size), 1.0, 0.0).astype(BF)
    count = width * size
    sums = [
        jnp.sum(hid[r * width : (r + 1) * width, :] + temb[r], axis=0, keepdims=True)
        for r in range(reqs)
    ]
    pad = [jnp.zeros((8 - reqs, chans), F32)] if reqs < 8 else []
    mean = sum_dot(jnp.concatenate(sums + pad, axis=0), member, ((1,), (0,))) / count
    wide = sum_dot(mean, member, ((1,), (1,)))
    squares = []
    for r in range(reqs):
        c = hid[r * width : (r + 1) * width, :] + temb[r] - wide[r : r + 1, :]
        squares.append(jnp.sum(c * c, axis=0, keepdims=True))
    second = sum_dot(jnp.concatenate(squares + pad, axis=0), member, ((1,), (0,)))
    stat_out[0] = mean
    stat_out[1] = second

    def st_copy(peer, src):
        return remote(stat_out, stat_in.at[src], st_s.at[peer], st_r.at[src], {"patch": peer})

    for k in range(1, n):
        st_copy((me + k) % n, me).start()
    stat_in[me] = stat_out[...]
    u_own.wait()
    u_side.wait_recv()

    @pl.when(z < top)
    def _():
        u_col(0, z).start()

    @pl.when(z > 0)
    def _():
        u_col(1, z).start()

    for k in range(1, n):
        st_copy((me + k) % n, (me + k) % n).wait_recv()
    means = stat_in[:, 0]
    total_mean = jnp.sum(means, axis=0) / n
    spread = means - total_mean[None]
    var = (jnp.sum(stat_in[:, 1], axis=0) + count * jnp.sum(spread * spread, axis=0)) / (count * n)
    mean_w = sum_dot(total_mean, member, ((1,), (1,)))
    inv_w = sum_dot(lax.rsqrt(var + 1e-05), member, ((1,), (1,)))
    scale = gain[...].reshape(1, chans)
    shift = bias[...].reshape(1, chans)
    for r in range(reqs):
        at = slice(r * width, (r + 1) * width)
        v = (hid[at, :] + temb[r] - mean_w[r : r + 1, :]) * inv_w[r : r + 1, :]
        v = v * scale + shift
        rows[z, at, :] = (v / (1.0 + jnp.exp(-v))).astype(BF)

    spans = (
        ((chans - win, win), (half, half - win), (0, half)),
        ((0, win), (win, half - win), (half, half)),
    )

    def a_copy(way, s, m):
        block = rows.at[s, :, pl.ds(*spans[way][m])]
        to = {"patch": me + 2 - 4 * way}
        return remote(block, block, a_s.at[way, s, m], a_r.at[s, m], to)

    def back(way, k):
        return z + k if way else z - k

    def hop(way, k, m):
        a_copy(way, back(way, k), m).wait_recv()

        @pl.when(middle)
        def _():
            a_copy(way, back(way, k), m).start()

    def x_fwd(s):
        return remote(rows.at[s, :, pl.ds(lane, win)], xin.at[s], xf_s.at[s], xf_r.at[s], side)

    px = lax.broadcasted_iota(jnp.int32, (cells, win), 0) % width

    def lay(y, v):
        v = v.astype(F32)
        taps[y + 1, :, 0:win] = jnp.where(px == 0, 0.0, pltpu.roll(v, 1, 0)).astype(BF)
        taps[y + 1, :, win : 2 * win] = v.astype(BF)
        taps[y + 1, :, 2 * win :] = jnp.where(px == width - 1, 0.0, pltpu.roll(v, cells - 1, 0)).astype(BF)

    def got(s):
        x_fwd(s).start()
        lay(2 * s + x, rows[s, :, pl.ds(lane, win)])

    def share_weights():
        @pl.when(hub)
        def _():
            for t in range(3):
                w_side(t).wait_recv()
                w_part(t, part).start()
                w_pass(t, part).start()

    def send_down(at, lo, hi):
        @pl.loop(lo, hi)
        def _(t):
            for copy in d_side(at, t):
                copy.start()

    end = jnp.logical_or(z == 0, z == top)
    middle = jnp.logical_not(end)

    @pl.when(z < top)
    def _():
        a_copy(0, z, 0).start()

    @pl.when(z > 0)
    def _():
        a_copy(1, z, 0).start()

    got(z)
    taps[0] = jnp.zeros(taps.shape[1:], BF)
    taps[n + 1] = jnp.zeros(taps.shape[1:], BF)

    def at_end(at, way):
        for m in (1, 2):
            a_copy(1 - way, z, m).start()
        for k in range(1, zs):
            hop(way, k, 0)
            got(back(way, k))
            if k == 1:
                share_weights()
        send_down(at, 0, 9)

    def at_middle(at, way):
        send_down(at, 0, 3)
        hop(1 - way, 1, 0)
        hop(way, 1, 0)
        a_copy(way, z, 1).start()
        share_weights()
        hop(1 - way, 2, 0)
        a_copy(1 - way, z, 1).start()
        hop(way, 1, 1)
        for k in (1, 2):
            hop(1 - way, k, 1)
            got(back(1 - way, k))
        for to in (way, 1 - way):
            a_copy(to, z, 2).start()
        hop(way, 1, 2)
        got(back(way, 1))
        send_down(at, 3, 9)

    for at, place, way in ((0, at_end, 1), (1, at_middle, 0), (2, at_middle, 1), (3, at_end, 0)):
        @pl.when(z == at)
        def _(place=place, at=at, way=way):
            place(at, way)

    @pl.when(hub)
    def _():
        for t in range(3):
            w_part(t, 1 - part).wait_recv()
            w_pass(t, 1 - part).start()

    @pl.loop(0, zs)
    def _(s):
        x_fwd(s).wait_recv()
        lay(2 * s + other, xin[s])

    @pl.when(hub)
    def _():
        for t in range(3):
            w_local(t).wait()

    @pl.when(jnp.logical_not(hub))
    def _():
        for t in range(3):
            w_twin(t).wait_recv()
            w_pass(t, 0).wait_recv()
            w_pass(t, 1).wait_recv()

    order = (3 * (1 - z // 2), (2 + 3 * z) % 5, 1 + z % 2, z)

    def conv(dest):
        for lo in range(0, half, WIN):
            hi = min(lo + WIN, half)
            s = jnp.zeros((2 * cells, hi - lo), F32)
            for dy in range(3):
                lhs = taps[pl.ds(2 * dest + dy, 2)].reshape(2 * cells, 3 * win)
                rhs = wpad[dy, :, :, lo:hi].reshape(3 * win, hi - lo)
                s += jnp.dot(lhs, rhs, preferred_element_type=F32)
            keep[dest, :, :, lo:hi] = s.reshape(2, cells, hi - lo)

    def z_copy(dest, a):
        after = jnp.where(dest > z, z + 1, z - 1)
        at = jnp.where(jnp.logical_and(dest < z, after == dest), zs, dest)
        return remote(
            zsend.at[dest, a], zrecv.at[at, a], z_s.at[dest, a], z_r.at[at, a], {"patch": after * 2 + x}
        )

    def z_arrival(at, a):
        return pltpu.make_async_copy(zrecv.at[at, a], zrecv.at[at, a], z_r.at[at, a])

    def push(dest, a):
        upward = jnp.logical_and(dest > z, z > 0)
        downward = jnp.logical_and(dest < z, z < top)

        @pl.when(jnp.logical_or(upward, downward))
        def _():
            z_arrival(dest, a).wait()
            keep[dest, a] += zrecv[dest, a].astype(F32)

        zsend[dest, a] = keep[dest, a].astype(BF)
        z_copy(dest, a).start()

    def conv_row(dest, a):
        for lo in range(0, half, WIN):
            hi = min(lo + WIN, half)
            s = jnp.zeros((cells, hi - lo), F32)
            for dy in range(3):
                rhs = wpad[dy, :, :, lo:hi].reshape(3 * win, hi - lo)
                s += jnp.dot(taps[2 * dest + a + dy], rhs, preferred_element_type=F32)
            keep[dest, a, :, lo:hi] = s

    for i in range(zs):
        if i == 0:
            conv_row(order[0], other)

            @pl.when(end)
            def _():
                push(order[0], other)

            conv_row(order[0], x)
        else:
            conv(order[i])
        if i < 2:
            for at, way in ((1, 1), (2, 0)):
                @pl.when(z == at)
                def _(i=i, way=way):
                    hop(way, i + 1, 2)

            @pl.when(middle)
            def _(i=i):
                u_hop(i + 1)
        if i == 0:
            @pl.when(middle)
            def _():
                push(order[0], other)
        elif i < zs - 1:
            push(order[i], other)
        if i < zs - 1:
            if i < zs - 2:
                push(order[i], x)

    @pl.when(end)
    def _():
        u_hop(1)
        u_hop(2)

    for at, way in ((0, 1), (top, 0)):
        @pl.when(z == at)
        def _(way=way):
            for k in range(1, zs):
                for m in (1, 2):
                    a_copy(way, back(way, k), m).wait_recv()

    for dx in range(3):
        for at in range(zs):
            @pl.when(z == at)
            def _(at=at, dx=dx):
                @pl.loop(3 * dx, 3 * dx + 3)
                def _(t):
                    for copy in d_side(at, t):
                        copy.wait_recv()

        d_pass(core, dx).start()
    for a in range(per):
        @pl.loop(0, 9)
        def _(t, a=a):
            d_own(a, t).wait()

    u_hop(3)

    def u_twin(at):
        part = uall.at[:, pl.ds(pl.multiple_of(at * hrank, hrank), hrank), :]
        return remote(part, part, up_s, up_r, twin)

    u_twin(core).start()
    for dx in range(3):
        d_pass(mate, dx).wait_recv()

    pq = lax.broadcasted_iota(jnp.int32, (zs * width, 3 * rank), 0) % width
    none = jnp.zeros((1, width, rank), F32)

    def products(lhs, rhs):
        prod = [
            lax.dot_general(lhs, rhs(dx), (((1,), (1,)), ((), ())), preferred_element_type=F32)
            for dx in range(3)
        ]
        s = prod[1]
        s += jnp.where(pq == 0, 0.0, pltpu.roll(prod[0], 1, 0))
        s += jnp.where(pq == width - 1, 0.0, pltpu.roll(prod[2], zs * width - 1, 0))
        s = s.reshape(zs, width, 3 * rank)
        above, level, below = s[:, :, :rank], s[:, :, rank : 2 * rank], s[:, :, 2 * rank :]
        even = above + jnp.concatenate([below[1:], none], axis=0)
        odd = jnp.concatenate([none, above[:-1]], axis=0) + below
        return level, even, odd

    for q in range(reqs // 2):
        pair_mine, pair_side = [], []
        for r in (2 * q, 2 * q + 1):
            stored = sel[r] - z * 2 * per
            here = jnp.logical_and(stored >= 0, stored < 2 * per)
            index = jnp.clip(stored, 0, 2 * per - 1)
            at = slice(r * width, (r + 1) * width)
            level, even, odd = products(
                rows[:, at, :].reshape(zs * width, chans), lambda dx: dall[index, dx]
            )
            level2, even2, odd2 = products(
                xin[:, at, :].reshape(zs * width, win), lambda dx: dall[index, dx, :, pl.ds(lane, win)]
            )
            first = x == 0
            pair_mine.append(jnp.where(here, level + jnp.where(first, odd2, even2), 0.0))
            pair_side.append(jnp.where(here, level2 + jnp.where(first, even, odd), 0.0))
        at = slice(q * width, (q + 1) * width)
        mine[:, at, :] = jnp.concatenate(pair_mine, axis=2)
        lxs[:, at, :] = jnp.concatenate(pair_side, axis=2).astype(BF)

    lx_copy = remote(lxs, lxr, lx_s, lx_r, side)
    lx_copy.start()

    def lz_copy(peer, src):
        return remote(lzs.at[peer // 2], lzr.at[src], lz_s.at[peer], lz_r.at[src], {"patch": peer})

    lx_copy.wait_recv()
    lzs[...] = (mine[...] + lxr[...].astype(F32)).astype(BF)
    for k in range(1, n):
        lz_copy((me + k) % n, me).start()

    push(order[zs - 2], x)
    lzr[me] = lzs[z]
    for k in range(1, n):
        lz_copy((me + k) % n, (me + k) % n).wait_recv()
    for a in range(2):
        low = lzr[a].astype(F32)
        for k in range(1, zs):
            low += lzr[2 * k + a].astype(F32)
        lows[a] = low.astype(BF)
    u_twin(mate).wait_recv()

    def f_copy(p):
        at = pl.ds(p * (cells // 2), cells // 2)
        return remote(fsend.at[at], frecv.at[at], f_s.at[p], f_r.at[p], side)

    for a in (other, x):
        for r in range(reqs):
            low = lows[a, r // 2 * width : (r // 2 + 1) * width, r % 2 * rank : (r % 2 + 1) * rank]
            at = slice(r * width, (r + 1) * width)
            keep[z, a, at, :] += jnp.dot(low, uall[sel[r]], preferred_element_type=F32)

        @pl.when(z > 0)
        def _(a=a):
            z_arrival(z, a).wait()
            keep[z, a] += zrecv[z, a].astype(F32)

        @pl.when(z < top)
        def _(a=a):
            z_arrival(zs, a).wait()
            keep[z, a] += zrecv[zs, a].astype(F32)

        if a is other:
            for p in range(2):
                at = slice(p * (cells // 2), (p + 1) * (cells // 2))
                fsend[at] = keep[z, other, at].astype(BF)
                f_copy(p).start()

    out[:, pl.ds(pl.multiple_of(x * half, LANES), half)] = keep[z, x]
    for p in range(2):
        at = slice(p * (cells // 2), (p + 1) * (cells // 2))
        f_copy(p).wait_recv()
        out[at, pl.ds(pl.multiple_of(other * half, LANES), half)] = frecv[at].astype(F32)

    for p in range(2):
        f_copy(p).wait_send()
    lx_copy.wait_send()
    for dx in range(3):
        d_pass(core, dx).wait_send()
    u_twin(core).wait_send()
    u_side.wait_send()
    for k in range(1, n):
        st_copy((me + k) % n, me).wait_send()
        lz_copy((me + k) % n, me).wait_send()

    for at in range(zs):
        @pl.when(z == at)
        def _(at=at):
            @pl.loop(0, 9)
            def _(t):
                for copy in d_side(at, t):
                    copy.wait_send()

    @pl.when(hub)
    def _():
        for t in range(3):
            w_twin(t).wait_send()
            w_part(t, part).wait_send()
            w_pass(t, 0).wait_send()
            w_pass(t, 1).wait_send()

    @pl.when(jnp.logical_not(hub))
    def _():
        for t in range(3):
            w_side(t).wait_send()

    @pl.loop(0, zs)
    def _(s):
        x_fwd(s).wait_send()

        @pl.when(jnp.logical_and(s <= z, z < top))
        def _():
            u_col(0, s).wait_send()

        @pl.when(jnp.logical_and(s >= z, z > 0))
        def _():
            u_col(1, s).wait_send()

        for h in range(3):
            @pl.when(jnp.logical_and(s <= z, z < top))
            def _(h=h):
                a_copy(0, s, h).wait_send()

            @pl.when(jnp.logical_and(s >= z, z > 0))
            def _(h=h):
                a_copy(1, s, h).wait_send()

        @pl.when(s != z)
        def _():
            for a in range(2):
                z_copy(s, a).wait_send()


def run_block(n, steps, asked, row_of, hid, table, gain, bias, weight, down, up):
    cells, chans = hid.shape
    reqs = asked.shape[0]
    width = cells // reqs
    own = weight.shape[1]
    per, rank, _ = down.shape
    zs = n // 2
    half = chans // 2
    win = -(-2 * own // LANES) * LANES
    dma = pltpu.SemaphoreType.DMA
    vmem = pl.BlockSpec(memory_space=pltpu.VMEM)
    hbm = pl.BlockSpec(memory_space=pl.ANY)
    smem = pl.BlockSpec(memory_space=pltpu.SMEM)
    low = (cells // 2, 2 * rank)
    return pl.pallas_call(
        functools.partial(block_kernel, n, own, reqs, width, chans),
        out_shape=jax.ShapeDtypeStruct((cells, chans), F32),
        in_specs=[smem] * 3 + [vmem] * 4 + [hbm] * 3,
        out_specs=vmem,
        scratch_shapes=[
            pltpu.VMEM((zs, cells, chans), BF),
            pltpu.VMEM((zs, cells, win), BF),
            pltpu.VMEM((n + 2, cells, 3 * win), BF),
            pltpu.VMEM((3, 3, win, half), BF),
            pltpu.VMEM((2 * per, 3, 3 * rank, chans), BF),
            pltpu.VMEM((n * per, rank, half), BF),
            pltpu.VMEM((2, 8, LANES), F32),
            pltpu.VMEM((n, 2, 8, LANES), F32),
            pltpu.VMEM((zs, 2, cells, half), F32),
            pltpu.VMEM((zs, 2, cells, half), BF),
            pltpu.VMEM((zs + 1, 2, cells, half), BF),
            pltpu.VMEM((cells, half), BF),
            pltpu.VMEM((cells, half), BF),
            pltpu.VMEM((zs,) + low, F32),
            pltpu.VMEM((zs,) + low, BF),
            pltpu.VMEM((zs,) + low, BF),
            pltpu.VMEM((zs,) + low, BF),
            pltpu.VMEM((n,) + low, BF),
            pltpu.VMEM((2,) + low, BF),
            dma((n,)), dma((n,)),
            dma((3, 3)), dma((3, 3)), dma((3,)), dma((3,)), dma((3,)), dma((3,)), dma((3,)),
            dma((9, 2)), dma((9, 2)), dma((per, 9)), dma((3,)), dma((3,)),
            dma, dma, dma, dma((2, zs)), dma((zs,)), dma, dma,
            dma((2, zs, 3)), dma((zs, 3)), dma((zs,)), dma((zs,)),
            dma((zs, 2)), dma((zs + 1, 2)),
            dma, dma, dma((n,)), dma((n,)), dma((2,)), dma((2,)),
        ],
        compiler_params=pltpu.CompilerParams(
            collective_id=0, has_side_effects=True, vmem_limit_bytes=56 * 2**20
        ),
        cost_estimate=pl.CostEstimate(
            flops=2 * n * cells * 9 * win * half, bytes_accessed=10**8, transcendentals=0
        ),
    )(steps, asked, row_of, hid, table, gain, bias, weight.reshape((3, 3) + weight.shape[1:]), down, up)


def split_contraction(
    hidden, skip, timestep_embedding_table, timesteps, group_norm_gain, group_norm_bias,
    kernel_weight, adapter_down_weight, adapter_up_weight, request_adapter, adapter_row_table,
):
    shape = hidden.shape
    flat = (shape[0] * shape[1] * shape[2], shape[3])
    total = run_block(
        lax.axis_size("patch"), timesteps, request_adapter, adapter_row_table,
        hidden.reshape(flat), timestep_embedding_table, group_norm_gain, group_norm_bias,
        kernel_weight, adapter_down_weight, adapter_up_weight,
    )
    return skip + total.reshape(shape)


def fits(n, hidden, kernel_weight, down):
    own = kernel_weight.shape[1]
    return (
        n == 8 and hidden.shape[1] == 1 and hidden.shape[0] in (2, 4, 6, 8)
        and hidden.shape[3] == 1280 and own == 160 and down.shape[:2] == (2, 64)
    )


def broadcast(block, axis, owner):
    block = jnp.where(lax.axis_index(axis) == owner, block, jnp.zeros_like(block))
    return lax.psum(block, axis)


def padded(cells, sides, width):
    for axis, dim in sides:
        count = lax.axis_size(axis)
        ends = count - 1
        head = lax.slice_in_dim(cells, 0, width, axis=dim)
        tail = lax.slice_in_dim(cells, cells.shape[dim] - width, cells.shape[dim], axis=dim)
        cells = jnp.concatenate(
            [
                lax.ppermute(tail, axis, [(i, (i + 1) % count) for i in range(ends)]),
                cells,
                lax.ppermute(head, axis, [((i + 1) % count, i) for i in range(ends)]),
            ],
            axis=dim,
        )
    return cells


def from_partner(x, axis, stride):
    return lax.ppermute(x, axis, [(i, i ^ 1 << stride) for i in range(lax.axis_size(axis))])


def make_taps(extended, rows, width):
    pieces = [extended[:, dy : dy + rows, dx : dx + width, :] for dy in range(3) for dx in range(3)]
    stacked = jnp.stack(pieces, axis=3)
    count = stacked.shape[0] * rows * width
    return stacked.reshape(count, 9, stacked.shape[-1])


def load_adapter_factors(
    adapter_down_weight, adapter_up_weight, request_adapter, adapter_row_table, request_total
):
    resident_count = adapter_down_weight.shape[0]
    fetched = []
    for request in range(request_total):
        resident_row = adapter_row_table[request_adapter[request]]
        owner = resident_row // resident_count
        store_position = resident_row % resident_count
        resident_down = lax.dynamic_index_in_dim(
            adapter_down_weight, store_position, 0, keepdims=False
        )
        resident_up = lax.dynamic_index_in_dim(adapter_up_weight, store_position, 0, keepdims=False)
        fetched.append(
            (broadcast(resident_down, "patch", owner), broadcast(resident_up, "patch", owner))
        )
    return fetched


def shards(
    hidden,
    skip,
    timestep_embedding_table,
    timesteps,
    group_norm_gain,
    group_norm_bias,
    kernel_weight,
    adapter_down_weight,
    adapter_up_weight,
    request_adapter,
    adapter_row_table,
):
    request_total, rows, width, chans = hidden.shape
    steps_count = timestep_embedding_table.shape[0]
    onehot = (timesteps[:, None] == jnp.arange(steps_count, dtype=jnp.int32)[None, :]).astype(
        jnp.float32
    )
    temb = jnp.dot(
        onehot,
        timestep_embedding_table,
        preferred_element_type=jnp.float32,
        precision=lax.Precision.HIGHEST,
    )
    shifted = hidden + temb[:, None, None, :]
    grouped = shifted.reshape(request_total, rows, width, GROUPS, chans // GROUPS)
    count = rows * lax.axis_size("patch") * width * (chans // GROUPS)
    totals = lax.psum(jnp.sum(grouped, axis=(1, 2, 4)), "patch")
    mean = totals / count
    centered = grouped - mean[:, None, None, :, None]
    squares = lax.psum(jnp.sum(centered * centered, axis=(1, 2, 4)), "patch")
    var = squares / count
    normed = (centered * lax.rsqrt(var + 1e-05)[:, None, None, :, None]).reshape(
        request_total, rows, width, chans
    )
    act = jax.nn.silu(normed * group_norm_gain + group_norm_bias).astype(jnp.bfloat16)
    extended = padded(act, (("patch", 1),), 1)
    extended = jnp.pad(extended, ((0, 0), (0, 0), (1, 1), (0, 0)))
    partner = from_partner(extended, "req", 0)
    taps = make_taps(jnp.concatenate([extended, partner], axis=0), rows, width)
    pixels = request_total * rows * width
    conv_half = jnp.einsum(
        "ptc,tco->po",
        taps,
        lax.all_gather(kernel_weight, "patch", axis=1, tiled=True),
        preferred_element_type=jnp.float32,
    )
    own_half = conv_half[:pixels]
    returned = from_partner(conv_half[pixels:], "req", 0)
    first = lax.axis_index("req") == 0
    left_half = jnp.where(first, own_half, returned)
    right_half = jnp.where(first, returned, own_half)
    conv = jnp.concatenate([left_half, right_half], axis=1).reshape(
        request_total, rows * width, chans
    )
    own_taps = taps[:pixels].reshape(request_total, rows * width, 9 * chans)
    adapter_factors = load_adapter_factors(
        adapter_down_weight, adapter_up_weight, request_adapter, adapter_row_table, request_total
    )
    deltas = []
    for request in range(request_total):
        down_factor, upper_limit = adapter_factors[request]
        low = lax.dot_general(
            own_taps[request],
            down_factor,
            (((1,), (1,)), ((), ())),
            preferred_element_type=jnp.float32,
        ).astype(jnp.bfloat16)
        deltas.append(jnp.dot(low, upper_limit, preferred_element_type=jnp.float32))
    total = conv + jnp.stack(deltas, axis=0)
    return skip + total.reshape(request_total, rows, width, chans)


def solution(mesh):
    def step(*args):
        n = lax.axis_size("patch")
        if fits(n, args[0], args[6], args[7]):
            return split_contraction(*args)
        return shards(*args)

    return jax.shard_map(
        step,
        mesh=mesh,
        in_specs=(
            P(("groups", "req"), "patch", None, None),
            P(("groups", "req"), "patch", None, None),
            P(),
            P(("groups", "req")),
            P(),
            P(),
            P(None, "patch", "req"),
            P(("groups", "patch"), None, None),
            P(("groups", "patch"), None, None),
            P(("groups", "req")),
            P("groups"),
        ),
        out_specs=P(("groups", "req"), "patch", None, None),
        check_vma=False,
    )
```
